256 devices in a mesh: replica: 32 (over x_lo, z, core), tensor: 8 (over y, x_hi).
Axes of the slice: x: 4 (x_hi: 2, x_lo: 2; x = x_hi * 2 + x_lo), y: 4, z: 8, core: 2. Of those that a mesh axis runs over, the one named last changes fastest.
Arguments:
- inputs: bfloat16 [2, 16384, 2048], P(None, 'replica', 'tensor'), may hold values from -6 to 6
- out_grads: bfloat16 [2, 16384, 2048], P(None, 'replica', 'tensor'), may hold values from -6 to 6
- gate_weight: bfloat16 [32, 2048, 2816], P('replica', None, 'tensor'), may hold values from -0.125 to 0.125
- up_weight: bfloat16 [32, 2048, 2816], P('replica', None, 'tensor'), may hold values from -0.125 to 0.125
- down_weight: bfloat16 [32, 2816, 2048], P('replica', 'tensor'), may hold values from -0.109375 to 0.109375
- rates: float32 [32], P('replica'), may hold values from 16 to 64
- partner_bits: int32 [4], replicated, may hold values from 0 to 3, each once
Outputs:
- new_gate: bfloat16 [32, 2048, 2816], P('replica', None, 'tensor')
- new_up: bfloat16 [32, 2048, 2816], P('replica', None, 'tensor')
- new_down: bfloat16 [32, 2816, 2048], P('replica', 'tensor')
- activations: bfloat16 [2, 16384, 2048], P(None, 'replica', 'tensor')
The draws below stay inside these ranges and needn't reach their ends.
Inputs may be any that keep to these rules, and one draw needn't show every extreme that they name: partner_bits holds each of the bit numbers 0, 1, 2, 3 exactly once; step s uses entry s.
All inputs are finite; a program needn't handle non-finite values.
Results may differ from the reference program's by a relative error of at most 0.024.
Values may be sent and summed in bfloat16 or wider, within the bound.
No kernel may reach another device: no remote copies, remote signals or barrier semaphores. Data moves between devices by JAX's collectives and lax.ppermute only.
A program may use at most 128 MiB of HBM per device.

```python
import math
import jax
import jax.numpy as jnp
from jax import lax

D = 2048
FF = 2816
TOK = 512
STEPS = 2
REPLICAS = 32
TOKENS = 16384


def levels(key, dims, shards, least, high):
    factor_of, own = 1.0, jax.random.fold_in(key, 6)
    for dim, parts in shards:
        draws = jnp.exp(jax.random.uniform(jax.random.fold_in(own, dim), (parts,), jnp.float32, least / len(shards), high / len(shards)))
        factor_of = factor_of * jnp.repeat(draws, dims[dim] // parts).reshape([-1 if axis == dim else 1 for axis in range(len(dims))])
    return factor_of


def normal_values(rng, shape, width, bound, shards=(), kind=jnp.bfloat16):
    level = levels(rng, shape, shards, -0.22, 0.18) if shards else 1.0
    drawn = jax.random.normal(rng, shape, jnp.float32) * width * level
    return jnp.minimum(jnp.maximum(drawn, -bound), bound).astype(kind)


def setup_inputs(seed: int = 0) -> dict:
    keys = jax.random.split(jax.random.key(seed), 8)
    inputs = normal_values(keys[0], (STEPS, TOKENS, D), 1.0, 6.0, ((1, 32), (2, 8)))
    out_grads = normal_values(keys[1], (STEPS, TOKENS, D), 1.0, 6.0, ((1, 32), (2, 8)))
    gate_weight = normal_values(keys[2], (REPLICAS, D, FF), D ** -0.5, 0.125, ((0, 32), (2, 8)))
    up_weight = normal_values(keys[3], (REPLICAS, D, FF), D ** -0.5, 0.125, ((0, 32), (2, 8)))
    down_weight = normal_values(keys[4], (REPLICAS, FF, D), FF ** -0.5, 0.109375, ((0, 32), (1, 8)))
    rates = jnp.clip(jnp.exp(math.log(64.0) - 1.3862944 * jax.random.uniform(keys[5], (REPLICAS,), jnp.float32) ** levels(keys[5], (REPLICAS,), ((0, 32),), -0.2, 0.2)), 16.0, 64.0)
    partner_bits = jax.random.permutation(keys[6], 4).astype(jnp.int32)
    return dict(inputs=inputs, out_grads=out_grads, gate_weight=gate_weight, up_weight=up_weight, down_weight=down_weight, rates=rates, partner_bits=partner_bits)


def local_pass(weights, inputs, grads_out):
    gate_w, up_w, down_w = weights
    gate = jnp.dot(inputs, gate_w, preferred_element_type=jnp.float32)
    up = jnp.dot(inputs, up_w, preferred_element_type=jnp.float32)
    sigma = jax.nn.sigmoid(gate)
    active = gate * sigma
    hidden = (active * up).astype(jnp.bfloat16)
    mixed = jnp.dot(hidden, down_w, preferred_element_type=jnp.float32)
    back = lax.dot_general(grads_out, down_w, (((1,), (1,)), ((), ())), preferred_element_type=jnp.float32)
    d_gate = (back * up * sigma * (1.0 + gate * (1.0 - sigma))).astype(jnp.bfloat16)
    d_up = (back * active).astype(jnp.bfloat16)
    grad_down = lax.dot_general(hidden, grads_out, (((0,), (0,)), ((), ())), preferred_element_type=jnp.float32)
    grad_gate = lax.dot_general(inputs, d_gate, (((0,), (0,)), ((), ())), preferred_element_type=jnp.float32)
    grad_up = lax.dot_general(inputs, d_up, (((0,), (0,)), ((), ())), preferred_element_type=jnp.float32)
    return (mixed, (grad_gate, grad_up, grad_down))

def squares_of(grads):
    return sum((jnp.sum(g * g) for g in grads))

def apply_update(weights, grads, squares, rate):
    scale = rate / jnp.sqrt(squares + 1e-06)
    return tuple(((w.astype(jnp.float32) - scale * g).astype(jnp.bfloat16) for w, g in zip(weights, grads)))

def average(first, second):
    return tuple((((a.astype(jnp.float32) + b.astype(jnp.float32)) * 0.5).astype(jnp.bfloat16) for a, b in zip(first, second)))

def reference(inputs, out_grads, gate_weight, up_weight, down_weight, rates, partner_bits):
    replica_ids = jnp.arange(REPLICAS, dtype=jnp.int32)
    weights = (gate_weight, up_weight, down_weight)
    results = []
    for step in range(STEPS):
        tokens = inputs[step].reshape(REPLICAS, TOK, D)
        grads_out = out_grads[step].reshape(REPLICAS, TOK, D)

        def one_replica(packed):
            gate_w, up_w, down_w, tok_rows, grad_rows, rate = packed
            mixed, grads = local_pass((gate_w, up_w, down_w), tok_rows, grad_rows)
            fresh = apply_update((gate_w, up_w, down_w), grads, squares_of(grads), rate)
            return (mixed.astype(jnp.bfloat16), fresh)
        mixed, fresh = lax.map(one_replica, (weights[0], weights[1], weights[2], tokens, grads_out, rates))
        partner = jnp.bitwise_xor(replica_ids, jnp.left_shift(jnp.int32(1), partner_bits[step].astype(jnp.int32)))
        other = tuple((jnp.take(f, partner, axis=0) for f in fresh))
        weights = average(fresh, other)
        results.append(mixed.reshape(TOKENS, D))
    return (weights[0], weights[1], weights[2], jnp.stack(results))
```

```python
from functools import partial

import jax
import jax.numpy as jnp
from jax import lax
from jax.sharding import PartitionSpec as P

AXES = ("replica", "tensor")
Y, XH = 4, 2


def tensor_permute(value, move):
    pairs = []
    for y in range(Y):
        for xh in range(XH):
            to_y, to_xh = move(y, xh)
            pairs.append((y * XH + xh, to_y % Y * XH + to_xh % XH))
    return lax.ppermute(value, "tensor", pairs)


def flip_x(value):
    return tensor_permute(value, lambda y, xh: (y, xh + 1))


def shift_y(value, by):
    return tensor_permute(value, lambda y, xh: (y + by, xh))


def flip_y(value, low):
    return tensor_permute(value, lambda y, xh: (y ^ 1 if low else 3 - y, xh))


def place(dy, dxh):
    me = lax.axis_index("tensor")
    return (me + dy * XH & Y * XH - XH) | ((me + dxh) & (XH - 1))


def gather(own):
    other = flip_x(own)
    both = jnp.stack([own, other])
    below = shift_y(both, 1)
    above = shift_y(both, -1)
    far0 = shift_y(below[0], 1)
    far1 = shift_y(above[1], -1)
    return [
        ((0, 0), own),
        ((0, 1), other),
        ((-1, 0), below[0]),
        ((-1, 1), below[1]),
        ((1, 0), above[0]),
        ((1, 1), above[1]),
        ((2, 0), far0),
        ((2, 1), far1),
    ]


def whole(pieces):
    rows, width = pieces[0][1].shape[-2:]
    lead = pieces[0][1].shape[:-1]
    out = jnp.zeros(lead + (width * Y * XH,), pieces[0][1].dtype)
    for (dy, dxh), piece in pieces:
        at = (0,) * len(lead) + (place(dy, dxh) * width,)
        out = lax.dynamic_update_slice(out, piece, at)
    return out


def scatter_sum(partial_sum):
    rows, columns = partial_sum.shape
    width = columns // (Y * XH)

    def block(dy, dxh):
        return lax.dynamic_slice(partial_sum, (0, place(dy, dxh) * width), (rows, width))

    def add(*parts):
        return sum(part.astype(jnp.float32) for part in parts).astype(partial_sum.dtype)

    from_below = shift_y(block(2, 0), 1)
    from_above = shift_y(block(2, 1), -1)
    up = shift_y(jnp.stack([add(block(1, 0), from_below), block(1, 1)]), 1)
    down = shift_y(jnp.stack([block(-1, 0), add(block(-1, 1), from_above)]), -1)
    across = flip_x(add(block(0, 1), up[1], down[1]))
    return add(block(0, 0), up[0], down[0], across)


def group_sum(value):
    value = jnp.full((8, 128), value)
    value = value + flip_x(value)
    value = value + flip_y(value, True)
    value = value + flip_y(value, False)
    return value[0, 0]


def contract(a, b, dim_a, dim_b):
    return lax.dot_general(
        a, b, (((dim_a,), (dim_b,)), ((), ())), preferred_element_type=jnp.float32
    )


def local_pass(weights, x, dy):
    gate_w, up_w, down_w = weights
    gate = contract(gate_w, x, 1, 1)
    up = contract(up_w, x, 1, 1)
    sigma = jax.nn.sigmoid(gate)
    active = gate * sigma
    hidden = (active * up).astype(jnp.bfloat16)
    mixed = contract(hidden, down_w, 0, 0).astype(jnp.bfloat16)
    back = contract(down_w, dy, 1, 1)
    d_gate = (back * up * sigma * (1.0 + gate * (1.0 - sigma))).astype(jnp.bfloat16)
    d_up = (back * active).astype(jnp.bfloat16)
    grads = (contract(d_gate, x, 1, 0), contract(d_up, x, 1, 0), contract(hidden, dy, 1, 0))
    return mixed, grads


def swap(bit, value):
    def branch(number, value):
        pairs = [(source, source ^ 2**number) for source in range(lax.axis_size("replica"))]
        return lax.ppermute(value, "replica", pairs)

    return lax.switch(bit, [partial(branch, number) for number in range(4)], value)


def local(inputs, out_grads, gate_weight, up_weight, down_weight, rates, partner_bits):
    weights = (gate_weight[0].T, up_weight[0].T, down_weight[0])
    steps = inputs.shape[0]
    gathered = []
    for step in range(steps):
        own = jnp.stack([inputs[step], out_grads[step]])
        if gathered:
            last = gathered[-1]
            held = lax.optimization_barrier((own, last[-2][1], last[-1][1]))
            own, last[-2:] = held[0], [(last[-2][0], held[1]), (last[-1][0], held[2])]
        gathered.append(gather(own))
    results = []
    for step in range(steps):
        x, dy = whole(gathered[step])
        mixed, grads = local_pass(weights, x, dy)
        squares = group_sum(sum(jnp.sum(g * g) for g in grads))
        scale = rates[0] / jnp.sqrt(squares + 1e-06)
        fresh = jnp.stack(
            [
                (w.astype(jnp.float32) - scale * g).astype(jnp.bfloat16)
                for w, g in zip(weights, grads)
            ]
        )
        other = swap(partner_bits[step], fresh)
        mean = (fresh.astype(jnp.float32) + other.astype(jnp.float32)) * 0.5
        weights = tuple(mean.astype(jnp.bfloat16))
        results.append(scatter_sum(mixed))
    return (weights[0].T[None], weights[1].T[None], weights[2][None], jnp.stack(results))


def solution(mesh):
    return jax.shard_map(
        local,
        mesh=mesh,
        in_specs=(
            P(None, "replica", "tensor"),
            P(None, "replica", "tensor"),
            P("replica", None, "tensor"),
            P("replica", None, "tensor"),
            P("replica", "tensor", None),
            P("replica"),
            P(),
        ),
        out_specs=(
            P("replica", None, "tensor"),
            P("replica", None, "tensor"),
            P("replica", "tensor", None),
            P(None, "replica", "tensor"),
        ),
        check_vma=False,
    )
```

```python
from functools import partial

import jax
import jax.numpy as jnp
from jax import lax
from jax.experimental import pallas as pl
from jax.experimental.pallas import tpu as pltpu
from jax.sharding import PartitionSpec as P

Y, XH = 4, 2
BF16, F32 = jnp.bfloat16, jnp.float32
ANY = pl.BlockSpec(memory_space=pl.ANY)
VMEM = pl.BlockSpec(memory_space=pltpu.VMEM)
SMEM = pl.BlockSpec(memory_space=pltpu.SMEM)


def tensor_permute(value, move):
    pairs = []
    for y in range(Y):
        for xh in range(XH):
            to_y, to_xh = move(y, xh)
            pairs.append((y * XH + xh, to_y % Y * XH + to_xh % XH))
    return lax.ppermute(value, "tensor", pairs)


def flip_x(value):
    return tensor_permute(value, lambda y, xh: (y, xh + 1))


def shift_y(value, by):
    return tensor_permute(value, lambda y, xh: (y + by, xh))


def flip_y(value, low):
    return tensor_permute(value, lambda y, xh: (y ^ 1 if low else 3 - y, xh))


def place(me, dy, dxh):
    return ((me + dy * XH) & (Y * XH - XH)) | ((me + dxh) & (XH - 1))


def gather(own):
    half = own.shape[0] // 2
    other = flip_x(own)
    below = shift_y(own, 1)
    above = shift_y(own, -1)
    up = shift_y(jnp.concatenate([other, below[:half]]), 1)
    down = shift_y(jnp.concatenate([other, above[half:]]), -1)
    far = jnp.concatenate([up[2 * half :], down[2 * half :]])
    return [own, other, below, above, up, down, far, flip_x(far)]


PIECES = [(0, 0), (0, 1), (-1, 0), (1, 0), (-1, 1), (1, 1), (2, 0), (2, 1)]


def fetch(me, pieces, out, sem):
    rows = out.shape[0]
    width = out.shape[1] // (Y * XH)
    copies = []
    for number, (piece, (dy, dxh)) in enumerate(zip(pieces, PIECES)):
        at = pl.multiple_of(place(me, dy, dxh) * width, width)
        copies.append(
            pltpu.make_async_copy(
                piece.at[pl.ds(0, rows)], out.at[:, pl.ds(at, width)], sem.at[number]
            )
        )
    for copy in copies:
        copy.start()
    return copies


def contract(a, b, dim_a, dim_b):
    return lax.dot_general(
        a, b, (((dim_a,), (dim_b,)), ((), ())), preferred_element_type=F32
    )


def forward_kernel(averaged, *refs):
    pieces, refs = refs[:8], refs[8:]
    if averaged:
        fresh, other, gate_out, up_out, hidden_out, mixed_out, x, weights, theirs, sems = refs
    else:
        *sources, gate_out, up_out, hidden_out, mixed_out, x, weights, sems = refs
    me = lax.axis_index("tensor")
    loads = []
    for number in range(3):
        if averaged:
            pair = [
                pltpu.make_async_copy(fresh.at[number], weights.at[number], sems.at[8 + number]),
                pltpu.make_async_copy(other.at[number], theirs.at[number], sems.at[11 + number]),
            ]
        else:
            pair = [
                pltpu.make_async_copy(sources[number], weights.at[number], sems.at[8 + number])
            ]
        for copy in pair:
            copy.start()
        loads.append(pair)
    copies = fetch(me, pieces, x, sems)

    def ready(number):
        for copy in loads[number]:
            copy.wait()
        if averaged:

            def mean(block, _):
                at = pl.ds(pl.multiple_of(block * 32, 32), 32)
                total = weights[number, at].astype(F32) + theirs[number, at].astype(F32)
                weights[number, at] = (total * 0.5).astype(BF16)
                return 0

            lax.fori_loop(0, weights.shape[1] // 32, mean, 0)

    ready(0)
    ready(1)
    for copy in copies:
        copy.wait()
    tokens = x.shape[0]
    chunk = 256

    def rows(block, _):
        at = pl.ds(pl.multiple_of(block * chunk, chunk), chunk)
        gate = contract(weights[0], x[at], 1, 1)
        up = contract(weights[1], x[at], 1, 1)
        gate_out[:, at] = gate
        up_out[:, at] = up
        hidden_out[:, at] = (gate * jax.nn.sigmoid(gate) * up).astype(BF16)
        return 0

    lax.fori_loop(0, tokens // chunk, rows, 0)
    ready(2)
    wide = 512

    def columns(block, _):
        at = pl.ds(pl.multiple_of(block * wide, wide), wide)
        mixed_out[:, at] = contract(hidden_out[...], weights[2, :, at], 0, 0).astype(BF16)
        return 0

    lax.fori_loop(0, x.shape[1] // wide, columns, 0)


def forward(pieces, weights, averaged):
    tokens, width = pieces[0].shape
    features = width * Y * XH
    hidden = weights[0].shape[-2]
    outs = [
        jax.ShapeDtypeStruct((hidden, tokens), F32),
        jax.ShapeDtypeStruct((hidden, tokens), F32),
        jax.ShapeDtypeStruct((hidden, tokens), BF16),
        jax.ShapeDtypeStruct((tokens, features), BF16),
        jax.ShapeDtypeStruct((tokens, features), BF16),
    ]
    specs = [VMEM] * 5
    scratch = [pltpu.SemaphoreType.DMA((14,))]
    stack = (3, hidden, features)
    if averaged:
        outs.append(jax.ShapeDtypeStruct(stack, BF16))
        specs.append(VMEM)
        scratch.insert(0, pltpu.VMEM(stack, BF16))
    else:
        scratch.insert(0, pltpu.VMEM(stack, BF16))
    size = tokens * features * hidden
    return pl.pallas_call(
        partial(forward_kernel, averaged),
        out_shape=outs,
        in_specs=[ANY] * (8 + len(weights)),
        out_specs=specs,
        scratch_shapes=scratch,
        name="forward",
        cost_estimate=pl.CostEstimate(
            flops=6 * size, bytes_accessed=12 << 20, transcendentals=hidden * tokens
        ),
    )(*pieces, *weights)


def backward_kernel(*refs):
    pieces, refs = refs[:8], refs[8:]
    x, gate_in, up_in, hidden, down, grads_out, squares_out, dy, d_gate, d_up, sems = refs
    me = lax.axis_index("tensor")
    copies = fetch(me, pieces, dy, sems)
    for copy in copies:
        copy.wait()
    tokens, features = dy.shape
    chunk = 256

    def rows(block, _):
        at = pl.ds(pl.multiple_of(block * chunk, chunk), chunk)
        back = contract(down[...], dy[at], 1, 1)
        gate = gate_in[:, at]
        sigma = jax.nn.sigmoid(gate)
        d_gate[:, at] = (
            back * up_in[:, at] * sigma * (1.0 + gate * (1.0 - sigma))
        ).astype(BF16)
        d_up[:, at] = (back * (gate * sigma)).astype(BF16)
        return 0

    lax.fori_loop(0, tokens // chunk, rows, 0)
    wide = 512

    def columns(block, total):
        at = pl.ds(pl.multiple_of(block * wide, wide), wide)
        for number, (left, right) in enumerate([(d_gate, x), (d_up, x), (hidden, dy)]):
            grad = contract(left[...], right[:, at], 1, 0)
            grads_out[number, :, at] = grad.astype(BF16)
            total = total + jnp.sum(grad * grad, axis=0, keepdims=True)
        return total

    total = lax.fori_loop(0, features // wide, columns, jnp.zeros((1, wide), F32))
    squares_out[...] = jnp.broadcast_to(jnp.sum(total, axis=1, keepdims=True), (8, 128))


def backward(pieces, x, gate, up, hidden, down):
    tokens, features = x.shape
    units = down.shape[0]
    size = tokens * features * units
    return pl.pallas_call(
        backward_kernel,
        out_shape=[
            jax.ShapeDtypeStruct((3, units, features), BF16),
            jax.ShapeDtypeStruct((8, 128), F32),
        ],
        in_specs=[ANY] * 8 + [VMEM] * 5,
        out_specs=[VMEM, VMEM],
        scratch_shapes=[
            pltpu.VMEM((tokens, features), BF16),
            pltpu.VMEM((units, tokens), BF16),
            pltpu.VMEM((units, tokens), BF16),
            pltpu.SemaphoreType.DMA((8,)),
        ],
        name="backward",
        cost_estimate=pl.CostEstimate(
            flops=8 * size, bytes_accessed=14 << 20, transcendentals=units * tokens
        ),
    )(*pieces, x, gate, up, hidden, down)


def update_kernel(scale, grads, *refs):
    *weights, out = refs
    for number in range(3):
        own = weights[number][...] if len(weights) == 3 else weights[0][number]
        out[number] = (own.astype(F32) - scale[0] * grads[number].astype(F32)).astype(BF16)


def update(scale, grads, weights):
    _, units, features = grads.shape
    rows = 32
    stack = pl.BlockSpec((3, rows, features), lambda i: (0, i, 0))
    flat = pl.BlockSpec((rows, features), lambda i: (i, 0))
    return pl.pallas_call(
        update_kernel,
        grid=(units // rows,),
        out_shape=jax.ShapeDtypeStruct(grads.shape, BF16),
        in_specs=[SMEM, stack] + [flat if w.ndim == 2 else stack for w in weights],
        out_specs=stack,
        name="update",
        cost_estimate=pl.CostEstimate(
            flops=2 * grads.size, bytes_accessed=6 * grads.size, transcendentals=0
        ),
    )(scale.reshape(1), grads, *weights)


def mean_kernel(fresh, other, *outs):
    for number in range(3):
        total = fresh[number].astype(F32) + other[number].astype(F32)
        outs[number][...] = (total * 0.5).astype(BF16)


def mean(fresh, other):
    _, units, features = fresh.shape
    rows = 32
    stack = pl.BlockSpec((3, rows, features), lambda i: (0, i, 0))
    flat = pl.BlockSpec((rows, features), lambda i: (i, 0))
    return pl.pallas_call(
        mean_kernel,
        grid=(units // rows,),
        out_shape=[jax.ShapeDtypeStruct((units, features), BF16)] * 3,
        in_specs=[stack, stack],
        out_specs=[flat] * 3,
        name="mean",
        cost_estimate=pl.CostEstimate(
            flops=2 * fresh.size, bytes_accessed=6 * fresh.size, transcendentals=0
        ),
    )(fresh, other)


def block(partial_sum, dy, dxh):
    width = partial_sum.shape[1] // (Y * XH)
    at = place(lax.axis_index("tensor"), dy, dxh) * width
    return lax.dynamic_slice(partial_sum, (0, at), (partial_sum.shape[0], width))


def add(*parts):
    return sum(part.astype(F32) for part in parts).astype(parts[0].dtype)


def scatter_first(value):
    return shift_y(block(value, 2, 0), 1), shift_y(block(value, 2, 1), -1)


def scatter_second(value, came):
    up = jnp.stack([add(block(value, 1, 0), came[0]), block(value, 1, 1)])
    down = jnp.stack([block(value, -1, 0), add(block(value, -1, 1), came[1])])
    return shift_y(up, 1), shift_y(down, -1)


def scatter_third(value, came):
    up, down = came
    return flip_x(add(block(value, 0, 1), up[1], down[1]))


def scatter_end(value, came, across):
    up, down = came
    return add(block(value, 0, 0), up[0], down[0], across)


def group_sum(value):
    value = value + flip_x(value)
    value = value + flip_y(value, True)
    value = value + flip_y(value, False)
    return value[0, 0]


def swap(bit, value):
    def branch(number, value):
        pairs = [(source, source ^ 2**number) for source in range(lax.axis_size("replica"))]
        return lax.ppermute(value, "replica", pairs)

    return lax.switch(bit, [partial(branch, number) for number in range(4)], value)


def after(value, *others):
    return lax.optimization_barrier((value, *others))[0]


def local(inputs, out_grads, gate_weight, up_weight, down_weight, rates, partner_bits):
    weights = (gate_weight[0].T, up_weight[0].T, down_weight[0])
    x1 = gather(inputs[0])
    dy1 = gather(out_grads[0])
    x2 = gather(after(inputs[1], x1[-1], dy1[5]))
    dy2 = gather(after(out_grads[1], x1[-1], dy1[5]))

    gate, up, hidden, mixed1, x = forward(x1, weights, False)
    grads, squares = backward(dy1, x, gate, up, hidden, weights[2])
    squares = group_sum(squares)
    scale = rates[0] / jnp.sqrt(squares + 1e-06)
    fresh = update(scale, grads, weights)
    fresh = after(fresh, x2[5], dy2[5])
    other = swap(partner_bits[0], fresh)

    first1 = scatter_first(mixed1)
    gate, up, hidden, mixed2, x, stack = forward(x2, (fresh, other), True)
    second1 = scatter_second(mixed1, first1)
    grads, squares = backward(dy2, x, gate, up, hidden, stack[2])
    first2 = scatter_first(mixed2)
    squares = group_sum(squares)
    scale = rates[0] / jnp.sqrt(squares + 1e-06)
    fresh = update(scale, grads, (stack,))
    third1 = scatter_third(mixed1, second1)
    second2 = scatter_second(mixed2, first2)
    other = swap(partner_bits[1], fresh)
    third2 = scatter_third(mixed2, second2)
    new = mean(fresh, other)
    results = [
        scatter_end(mixed1, second1, third1),
        scatter_end(mixed2, second2, third2),
    ]
    return (new[0].T[None], new[1].T[None], new[2][None], jnp.stack(results))


def solution(mesh):
    return jax.shard_map(
        local,
        mesh=mesh,
        in_specs=(
            P(None, "replica", "tensor"),
            P(None, "replica", "tensor"),
            P("replica", None, "tensor"),
            P("replica", None, "tensor"),
            P("replica", "tensor", None),
            P("replica"),
            P(),
        ),
        out_specs=(
            P("replica", None, "tensor"),
            P("replica", None, "tensor"),
            P("replica", "tensor", None),
            P(None, "replica", "tensor"),
        ),
        check_vma=False,
    )
```

```python
from functools import partial

import jax
import jax.numpy as jnp
from jax import lax
from jax.experimental import pallas as pl
from jax.experimental.pallas import tpu as pltpu
from jax.sharding import PartitionSpec as P

Y, XH = 4, 2
BF16, F32 = jnp.bfloat16, jnp.float32
ANY = pl.BlockSpec(memory_space=pl.ANY)
VMEM = pl.BlockSpec(memory_space=pltpu.VMEM)


def tensor_permute(value, move):
    pairs = []
    for y in range(Y):
        for xh in range(XH):
            to_y, to_xh = move(y, xh)
            pairs.append((y * XH + xh, to_y % Y * XH + to_xh % XH))
    return lax.ppermute(value, "tensor", pairs)


def flip_x(value):
    return tensor_permute(value, lambda y, xh: (y, xh + 1))


def shift_y(value, by):
    return tensor_permute(value, lambda y, xh: (y + by, xh))


def flip_y(value, low):
    return tensor_permute(value, lambda y, xh: (y ^ 1 if low else 3 - y, xh))


def place(me, dy, dxh):
    return ((me + dy * XH) & (Y * XH - XH)) | ((me + dxh) & (XH - 1))


def gather(own):
    half = own.shape[0] // 2
    other = flip_x(own)
    below = shift_y(own, 1)
    above = shift_y(own, -1)
    up = shift_y(jnp.concatenate([other, below[:half]]), 1)
    down = shift_y(jnp.concatenate([other, above[half:]]), -1)
    far = jnp.concatenate([up[2 * half :], down[2 * half :]])
    return [own, other, below, above, up, down, far, flip_x(far)]


def gather_near(own):
    return [flip_x(own), shift_y(own, 1), shift_y(own, -1), shift_y(own, 2)]


def gather_across(own, near):
    other, below, above, far = near
    return [own, other, below, above, far, flip_x(jnp.stack([below, above, far]))]


PIECES = [(0, 0), (0, 1), (-1, 0), (1, 0), (-1, 1), (1, 1), (2, 0), (2, 1)]


def fetch(me, pieces, first, out, sems):
    rows = out.shape[0]
    width = out.shape[1] // (Y * XH)
    copies = []
    for number, (piece, (dy, dxh)) in enumerate(zip(pieces, PIECES)):
        at = pl.multiple_of(place(me, dy, dxh) * width, width)
        copies.append(
            pltpu.make_async_copy(
                piece.at[pl.ds(first, rows)], out.at[:, pl.ds(at, width)], sems.at[number]
            )
        )
    for copy in copies:
        copy.start()
    return copies


def contract(a, b, dim_a, dim_b):
    return lax.dot_general(
        a, b, (((dim_a,), (dim_b,)), ((), ())), preferred_element_type=F32
    )


def step_kernel(averaged, *refs):
    if averaged:
        (own, flipped, below, above, far, across), (fresh, other, *refs) = refs[:6], refs[6:]
        pieces = [own, flipped, below, above, across.at[0], across.at[1], far, across.at[2]]
        x_pieces = dy_pieces = pieces
    else:
        x_pieces, dy_pieces, refs = refs[:8], refs[8:16], refs[16:]
        *sources, refs = refs[:3] + (refs[3:],)
    stack_out, grads_out, hidden, squares_out, *refs = refs
    weights, theirs, x, dy, grads, gates, ups, d_gate, d_up, x_sems, dy_sems, w_sems, o_sems = refs
    tokens, features = x.shape
    units = weights.shape[1]
    me = lax.axis_index("tensor")

    def load(number):
        if averaged:
            copies = [
                pltpu.make_async_copy(fresh.at[number], weights.at[number], w_sems.at[number]),
                pltpu.make_async_copy(other.at[number], theirs.at[number], w_sems.at[3 + number]),
            ]
        else:
            copies = [
                pltpu.make_async_copy(sources[number], weights.at[number], w_sems.at[number])
            ]
        for copy in copies:
            copy.start()
        return copies

    loads = [load(0)]
    x_copies = fetch(me, x_pieces, 0, x, x_sems)
    loads += [load(1), load(2)]
    dy_copies = fetch(me, dy_pieces, tokens if averaged else 0, dy, dy_sems)
    stores = []

    def ready(number):
        for copy in loads[number]:
            copy.wait()
        if averaged:

            def mean(block, _):
                at = pl.ds(pl.multiple_of(block * 32, 32), 32)
                total = weights[number, at].astype(F32) + theirs[number, at].astype(F32)
                weights[number, at] = (total * 0.5).astype(BF16)
                return 0

            lax.fori_loop(0, units // 32, mean, 0)
        stores.append(
            pltpu.make_async_copy(weights.at[number], stack_out.at[number], o_sems.at[number])
        )
        stores[-1].start()

    chunk = 256
    wide = 512

    def over_tokens(body):
        def step(block, _):
            body(pl.ds(pl.multiple_of(block * chunk, chunk), chunk))
            return 0

        lax.fori_loop(0, tokens // chunk, step, 0)

    def gate_pass(at):
        gates[:, at] = contract(weights[0], x[at], 1, 1)

    def up_pass(at):
        up = contract(weights[1], x[at], 1, 1)
        gate = gates[:, at]
        ups[:, at] = up
        hidden[:, at] = (gate * jax.nn.sigmoid(gate) * up).astype(BF16)

    def back_pass(at):
        back = contract(weights[2], dy[at], 1, 1)
        gate = gates[:, at]
        sigma = jax.nn.sigmoid(gate)
        d_gate[:, at] = (
            back * ups[:, at] * sigma * (1.0 + gate * (1.0 - sigma))
        ).astype(BF16)
        d_up[:, at] = (back * (gate * sigma)).astype(BF16)

    ready(0)
    for copy in x_copies:
        copy.wait()
    over_tokens(gate_pass)
    ready(1)
    over_tokens(up_pass)
    ready(2)
    for copy in dy_copies:
        copy.wait()
    over_tokens(back_pass)

    def grad_store(block):
        at = pl.ds(pl.multiple_of(block * wide, wide), wide)
        return pltpu.make_async_copy(
            grads.at[:, :, at], grads_out.at[:, :, at], o_sems.at[3 + block]
        )

    def columns(block, total):
        at = pl.ds(pl.multiple_of(block * wide, wide), wide)
        for number, (left, right) in enumerate([(d_gate, x), (d_up, x), (hidden, dy)]):
            grad = contract(left[...], right[:, at], 1, 0)
            grads[number, :, at] = grad.astype(BF16)
            total = total + jnp.sum(grad * grad, axis=0, keepdims=True)
        grad_store(block).start()
        return total

    blocks = features // wide
    total = lax.fori_loop(0, blocks, columns, jnp.zeros((1, wide), F32))
    squares_out[...] = jnp.broadcast_to(jnp.sum(total, axis=1, keepdims=True), (8, 128))
    for store in stores:
        store.wait()
    for block in range(blocks):
        grad_store(block).wait()


def step_pass(x_pieces, dy_pieces, weights):
    averaged = dy_pieces is None
    rows, width = x_pieces[0].shape
    tokens = rows // 2 if averaged else rows
    features = width * Y * XH
    units = weights[0].shape[-2]
    pieces = x_pieces if averaged else x_pieces + dy_pieces
    size = tokens * features * units
    stack = (3, units, features)
    return pl.pallas_call(
        partial(step_kernel, averaged),
        out_shape=[
            jax.ShapeDtypeStruct(stack, BF16),
            jax.ShapeDtypeStruct(stack, BF16),
            jax.ShapeDtypeStruct((units, tokens), BF16),
            jax.ShapeDtypeStruct((8, 128), F32),
        ],
        in_specs=[ANY] * (len(pieces) + len(weights)),
        out_specs=[ANY, ANY, VMEM, VMEM],
        scratch_shapes=[
            pltpu.VMEM(stack, BF16),
            pltpu.VMEM(stack if averaged else (8, 128), BF16),
            pltpu.VMEM((tokens, features), BF16),
            pltpu.VMEM((tokens, features), BF16),
            pltpu.VMEM(stack, BF16),
            pltpu.VMEM((units, tokens), F32),
            pltpu.VMEM((units, tokens), F32),
            pltpu.VMEM((units, tokens), BF16),
            pltpu.VMEM((units, tokens), BF16),
            pltpu.SemaphoreType.DMA((8,)),
            pltpu.SemaphoreType.DMA((8,)),
            pltpu.SemaphoreType.DMA((6,)),
            pltpu.SemaphoreType.DMA((3 + features // 512,)),
        ],
        name="step",
        cost_estimate=pl.CostEstimate(
            flops=12 * size, bytes_accessed=16 << 20, transcendentals=2 * units * tokens
        ),
    )(*pieces, *weights)


SENDS = [0, 1, -1, 2]


def outputs_kernel(hidden1, hidden2, stack1, stack2, *refs):
    outs, (hidden, down, sems) = refs[:4], refs[4:]
    me = lax.axis_index("tensor")
    pairs = [(hidden1, hidden.at[0]), (hidden2, hidden.at[1])]
    pairs += [(stack1.at[2], down.at[0]), (stack2.at[2], down.at[1])]
    loads = [
        pltpu.make_async_copy(source, to, sems.at[number])
        for number, (source, to) in enumerate(pairs)
    ]
    for load in loads:
        load.start()
    for load in loads:
        load.wait()
    tokens = hidden.shape[2]
    width = outs[0].shape[2]

    def part(index, _):
        number, dxh = index // 2, index % 2
        rows = pl.ds(pl.multiple_of(number * tokens, tokens), tokens)
        for out, dy in zip(outs, SENDS):
            at = pl.ds(pl.multiple_of(place(me, dy, dxh) * width, width), width)
            out[dxh, rows] = contract(hidden[number], down[number, :, at], 0, 0).astype(BF16)
        return 0

    lax.fori_loop(0, 4, part, 0)


def outputs(hidden1, hidden2, stack1, stack2):
    units, tokens = hidden1.shape
    features = stack1.shape[2]
    width = features // (Y * XH)
    return pl.pallas_call(
        outputs_kernel,
        out_shape=[jax.ShapeDtypeStruct((2, 2 * tokens, width), BF16)] * 4,
        in_specs=[ANY] * 4,
        out_specs=[VMEM] * 4,
        scratch_shapes=[
            pltpu.VMEM((2, units, tokens), BF16),
            pltpu.VMEM((2, units, features), BF16),
            pltpu.SemaphoreType.DMA((4,)),
        ],
        name="outputs",
        cost_estimate=pl.CostEstimate(
            flops=4 * tokens * features * units, bytes_accessed=8 << 20, transcendentals=0
        ),
    )(hidden1, hidden2, stack1, stack2)


def add(*parts):
    return sum(part.astype(F32) for part in parts).astype(parts[0].dtype)


def updated(rate, squares, stack, grads):
    scale = rate / jnp.sqrt(group_sum(squares) + 1e-06)
    return (stack.astype(F32) - scale * grads.astype(F32)).astype(BF16), scale


def group_sum(value):
    value = value + flip_x(value)
    value = value + flip_y(value, True)
    value = value + flip_y(value, False)
    return value[0, 0]


def swap(bit, value):
    def branch(number, value):
        pairs = [(source, source ^ 2**number) for source in range(lax.axis_size("replica"))]
        return lax.ppermute(value, "replica", pairs)

    return lax.switch(bit, [partial(branch, number) for number in range(4)], value)


def after(value, *others):
    return lax.optimization_barrier((value, *others))[0]


def local(inputs, out_grads, gate_weight, up_weight, down_weight, rates, partner_bits):
    weights = [gate_weight[0].T, up_weight[0].T, down_weight[0]]
    x1 = gather(inputs[0])
    dy1 = gather(out_grads[0])
    own2 = jnp.concatenate([inputs[1], out_grads[1]])
    own2 = after(own2, x1[4], x1[5], dy1[4], dy1[5])
    near2 = gather_near(own2)

    stack1, grads, hidden1, squares = step_pass(x1, dy1, weights)
    near2 = list(lax.optimization_barrier((*near2, squares))[:4])
    pieces2 = gather_across(own2, near2)
    fresh, _ = updated(rates[0], squares, stack1, grads)
    other = swap(partner_bits[0], fresh)

    stack2, grads, hidden2, squares = step_pass(pieces2, None, [fresh, other])
    blocks = outputs(hidden1, hidden2, stack1, stack2)
    fresh, scale = updated(rates[0], squares, stack2, grads)
    blocks = lax.optimization_barrier((*blocks, scale))[:4]
    came = [shift_y(part, by) for part, by in zip(blocks[1:], SENDS[1:])]
    other = swap(partner_bits[1], fresh)
    across = flip_x(add(blocks[0][1], *(part[1] for part in came)))
    new = [
        ((fresh[number].astype(F32) + other[number].astype(F32)) * 0.5).astype(BF16)
        for number in range(3)
    ]
    results = add(blocks[0][0], *(part[0] for part in came), across)
    return (new[0].T[None], new[1].T[None], new[2][None], results.reshape(inputs.shape))


def solution(mesh):
    return jax.shard_map(
        local,
        mesh=mesh,
        in_specs=(
            P(None, "replica", "tensor"),
            P(None, "replica", "tensor"),
            P("replica", None, "tensor"),
            P("replica", None, "tensor"),
            P("replica", "tensor", None),
            P("replica"),
            P(),
        ),
        out_specs=(
            P("replica", None, "tensor"),
            P("replica", None, "tensor"),
            P("replica", "tensor", None),
            P(None, "replica", "tensor"),
        ),
        check_vma=False,
    )
```

```python
from functools import partial

import jax
import jax.numpy as jnp
from jax import lax
from jax.experimental import pallas as pl
from jax.experimental.pallas import tpu as pltpu
from jax.sharding import PartitionSpec as P

Y, XH = 4, 2
BF16, F32 = jnp.bfloat16, jnp.float32
ANY = pl.BlockSpec(memory_space=pl.ANY)
VMEM = pl.BlockSpec(memory_space=pltpu.VMEM)
HBM = pl.BlockSpec(memory_space=pltpu.HBM)


def tensor_permute(value, move):
    pairs = []
    for y in range(Y):
        for xh in range(XH):
            to_y, to_xh = move(y, xh)
            pairs.append((y * XH + xh, to_y % Y * XH + to_xh % XH))
    return lax.ppermute(value, "tensor", pairs)


def flip_x(value):
    return tensor_permute(value, lambda y, xh: (y, xh + 1))


def shift_y(value, by):
    return tensor_permute(value, lambda y, xh: (y + by, xh))


def flip_y(value, low):
    return tensor_permute(value, lambda y, xh: (y ^ 1 if low else 3 - y, xh))


def place(me, dy, dxh):
    return ((me + dy * XH) & (Y * XH - XH)) | ((me + dxh) & (XH - 1))


def gather(own):
    below = shift_y(own, 1)
    above = shift_y(own, -1)
    other = flip_x(own)
    far = shift_y(own, 2)
    return [own, other, below, above, shift_y(other, 1), shift_y(other, -1), far, flip_x(far)]


def gather_near(own):
    return [flip_x(own), shift_y(own, 1), shift_y(own, -1), shift_y(own, 2)]


def gather_across(own, near):
    other, below, above, far = near
    return [own, other, below, above, far, flip_x(jnp.stack([below, above, far]))]


PIECES = [(0, 0), (0, 1), (-1, 0), (1, 0), (-1, 1), (1, 1), (2, 0), (2, 1)]


def fetch(me, pieces, first, out, sems):
    rows = out.shape[0]
    width = out.shape[1] // (Y * XH)
    copies = []
    for number, (piece, (dy, dxh)) in enumerate(zip(pieces, PIECES)):
        at = pl.multiple_of(place(me, dy, dxh) * width, width)
        copies.append(
            pltpu.make_async_copy(
                piece.at[pl.ds(first, rows)], out.at[:, pl.ds(at, width)], sems.at[number]
            )
        )
    for copy in copies:
        copy.start()
    return copies


def contract(a, b, dim_a, dim_b):
    return lax.dot_general(
        a, b, (((dim_a,), (dim_b,)), ((), ())), preferred_element_type=F32
    )


def step_kernel(averaged, *refs):
    if averaged:
        (own, flipped, below, above, far, across), (fresh, other, *refs) = refs[:6], refs[6:]
        pieces = [own, flipped, below, above, across.at[0], across.at[1], far, across.at[2]]
    else:
        pieces, sources, refs = refs[:8], refs[8:11], refs[11:]
    stack_out, grads_out, hidden, squares_out, *refs = refs
    weights, theirs, x, dy, grads, gates, ups, d_gate, d_up, x_sems, dy_sems, w_sems, o_sems = refs
    tokens, features = x.shape
    units = weights.shape[1]
    me = lax.axis_index("tensor")

    def load(number):
        if averaged:
            copies = [
                pltpu.make_async_copy(fresh.at[number], weights.at[number], w_sems.at[number]),
                pltpu.make_async_copy(other.at[number], theirs.at[number], w_sems.at[3 + number]),
            ]
        else:
            copies = [
                pltpu.make_async_copy(sources[number], weights.at[number], w_sems.at[number])
            ]
        for copy in copies:
            copy.start()
        return copies

    loads = [load(0)]
    x_copies = fetch(me, pieces, 0, x, x_sems)
    loads += [load(1), load(2)]
    dy_copies = fetch(me, pieces, tokens, dy, dy_sems)
    stores = []

    def ready(number):
        for copy in loads[number]:
            copy.wait()
        if averaged:

            def mean(block, _):
                at = pl.ds(pl.multiple_of(block * 32, 32), 32)
                total = weights[number, at].astype(F32) + theirs[number, at].astype(F32)
                weights[number, at] = (total * 0.5).astype(BF16)
                return 0

            lax.fori_loop(0, units // 32, mean, 0)
        stores.append(
            pltpu.make_async_copy(weights.at[number], stack_out.at[number], o_sems.at[number])
        )
        stores[-1].start()

    chunk = 256
    wide = 512

    def over_tokens(body):
        def step(block, _):
            body(pl.ds(pl.multiple_of(block * chunk, chunk), chunk))
            return 0

        lax.fori_loop(0, tokens // chunk, step, 0)

    def gate_pass(at):
        gates[:, at] = contract(weights[0], x[at], 1, 1)

    def up_pass(at):
        up = contract(weights[1], x[at], 1, 1)
        gate = gates[:, at]
        ups[:, at] = up
        hidden[:, at] = (gate * jax.nn.sigmoid(gate) * up).astype(BF16)

    def back_pass(at):
        back = contract(weights[2], dy[at], 1, 1)
        gate = gates[:, at]
        sigma = jax.nn.sigmoid(gate)
        d_gate[:, at] = (
            back * ups[:, at] * sigma * (1.0 + gate * (1.0 - sigma))
        ).astype(BF16)
        d_up[:, at] = (back * (gate * sigma)).astype(BF16)

    ready(0)
    for copy in x_copies:
        copy.wait()
    over_tokens(gate_pass)
    ready(1)
    over_tokens(up_pass)
    ready(2)
    for copy in dy_copies:
        copy.wait()
    over_tokens(back_pass)

    def grad_store(block):
        at = pl.ds(pl.multiple_of(block * wide, wide), wide)
        return pltpu.make_async_copy(
            grads.at[:, :, at], grads_out.at[:, :, at], o_sems.at[3 + block]
        )

    def columns(block, total):
        at = pl.ds(pl.multiple_of(block * wide, wide), wide)
        for number, (left, right) in enumerate([(d_gate, x), (d_up, x), (hidden, dy)]):
            grad = contract(left[...], right[:, at], 1, 0)
            grads[number, :, at] = grad.astype(BF16)
            total = total + jnp.sum(grad * grad, axis=0, keepdims=True)
        grad_store(block).start()
        return total

    blocks = features // wide
    total = lax.fori_loop(0, blocks, columns, jnp.zeros((1, wide), F32))
    squares_out[...] = jnp.broadcast_to(jnp.sum(total, axis=1, keepdims=True), (8, 128))
    for store in stores:
        store.wait()
    for block in range(blocks):
        grad_store(block).wait()


def step_pass(pieces, weights, averaged):
    rows, width = pieces[0].shape
    tokens = rows // 2
    features = width * Y * XH
    units = weights[0].shape[-2]
    size = tokens * features * units
    stack = (3, units, features)
    return pl.pallas_call(
        partial(step_kernel, averaged),
        out_shape=[
            pltpu.HBM(stack, BF16),
            pltpu.HBM(stack, BF16),
            jax.ShapeDtypeStruct((units, tokens), BF16),
            jax.ShapeDtypeStruct((8, 128), F32),
        ],
        in_specs=[ANY] * (len(pieces) + len(weights)),
        out_specs=[HBM, HBM, VMEM, VMEM],
        scratch_shapes=[
            pltpu.VMEM(stack, BF16),
            pltpu.VMEM(stack if averaged else (8, 128), BF16),
            pltpu.VMEM((tokens, features), BF16),
            pltpu.VMEM((tokens, features), BF16),
            pltpu.VMEM(stack, BF16),
            pltpu.VMEM((units, tokens), F32),
            pltpu.VMEM((units, tokens), F32),
            pltpu.VMEM((units, tokens), BF16),
            pltpu.VMEM((units, tokens), BF16),
            pltpu.SemaphoreType.DMA((8,)),
            pltpu.SemaphoreType.DMA((8,)),
            pltpu.SemaphoreType.DMA((6,)),
            pltpu.SemaphoreType.DMA((3 + features // 512,)),
        ],
        name="step",
        compiler_params=pltpu.CompilerParams(vmem_limit_bytes=28 << 20),
        cost_estimate=pl.CostEstimate(
            flops=12 * size, bytes_accessed=16 << 20, transcendentals=2 * units * tokens
        ),
    )(*pieces, *weights)


SENDS = [0, 1, -1, 2]


def outputs_kernel(hidden1, hidden2, down1, stack2, *refs):
    outs, (hidden, down, sems) = refs[:4], refs[4:]
    me = lax.axis_index("tensor")
    pairs = [(hidden1, hidden.at[0]), (hidden2, hidden.at[1])]
    pairs += [(down1, down.at[0]), (stack2.at[2], down.at[1])]
    loads = [
        pltpu.make_async_copy(source, to, sems.at[number])
        for number, (source, to) in enumerate(pairs)
    ]
    for load in loads:
        load.start()
    for load in loads:
        load.wait()
    tokens = hidden.shape[2]
    width = outs[0].shape[2]

    def part(index, _):
        number, dxh = index // 2, index % 2
        rows = pl.ds(pl.multiple_of(number * tokens, tokens), tokens)
        for out, dy in zip(outs, SENDS):
            at = pl.ds(pl.multiple_of(place(me, dy, dxh) * width, width), width)
            out[dxh, rows] = contract(hidden[number], down[number, :, at], 0, 0).astype(BF16)
        return 0

    lax.fori_loop(0, 4, part, 0)


def outputs(hidden1, hidden2, down1, stack2):
    units, tokens = hidden1.shape
    features = down1.shape[1]
    width = features // (Y * XH)
    return pl.pallas_call(
        outputs_kernel,
        out_shape=[jax.ShapeDtypeStruct((2, 2 * tokens, width), BF16)] * 4,
        in_specs=[ANY] * 4,
        out_specs=[VMEM] * 4,
        scratch_shapes=[
            pltpu.VMEM((2, units, tokens), BF16),
            pltpu.VMEM((2, units, features), BF16),
            pltpu.SemaphoreType.DMA((4,)),
        ],
        name="outputs",
        compiler_params=pltpu.CompilerParams(vmem_limit_bytes=16 << 20),
        cost_estimate=pl.CostEstimate(
            flops=4 * tokens * features * units, bytes_accessed=8 << 20, transcendentals=0
        ),
    )(hidden1, hidden2, down1, stack2)


def add(*parts):
    return sum(part.astype(F32) for part in parts).astype(parts[0].dtype)


def updated(rate, squares, stack, grads):
    scale = rate / jnp.sqrt(squares + 1e-06)
    return (stack.astype(F32) - scale * grads.astype(F32)).astype(BF16)


def group_sum(value):
    near = value + flip_x(value)
    value = near + flip_y(near, True)
    value = value + flip_y(value, False)
    return value[0, 0], near


def swap(bit, value):
    def branch(number, value):
        pairs = [(source, source ^ 2**number) for source in range(lax.axis_size("replica"))]
        return lax.ppermute(value, "replica", pairs)

    return lax.switch(bit, [partial(branch, number) for number in range(4)], value)


def after(value, *others):
    return lax.optimization_barrier((value, *others))[0]


def local(inputs, out_grads, gate_weight, up_weight, down_weight, rates, partner_bits):
    weights = [gate_weight[0].T, up_weight[0].T, down_weight[0]]
    own1 = jnp.concatenate([inputs[0], out_grads[0]])
    pieces1 = gather(own1)
    own2 = jnp.concatenate([inputs[1], out_grads[1]])
    own2 = after(own2, pieces1[4], pieces1[5])
    near2 = gather_near(own2)

    stack1, grads, hidden1, squares = step_pass(pieces1, weights, False)
    squares, flipped = group_sum(squares)
    near2 = list(lax.optimization_barrier((*near2, flipped))[:4])
    pieces2 = gather_across(own2, near2)
    fresh = updated(rates[0], squares, stack1, grads)
    other = swap(partner_bits[0], fresh)

    stack2, grads, hidden2, squares = step_pass(pieces2, [fresh, other], True)
    blocks = outputs(hidden1, hidden2, weights[2], stack2)
    squares, _ = group_sum(squares)
    fresh = updated(rates[0], squares, stack2, grads)
    blocks = lax.optimization_barrier((*blocks, squares))[:4]
    came = [shift_y(part, by) for part, by in zip(blocks[1:], SENDS[1:])]
    other = swap(partner_bits[1], fresh)
    across = flip_x(add(blocks[0][1], *(part[1] for part in came)))
    new = [
        ((fresh[number].astype(F32) + other[number].astype(F32)) * 0.5).astype(BF16)
        for number in range(3)
    ]
    results = add(blocks[0][0], *(part[0] for part in came), across)
    return (new[0].T[None], new[1].T[None], new[2][None], results.reshape(inputs.shape))


def solution(mesh):
    return jax.shard_map(
        local,
        mesh=mesh,
        in_specs=(
            P(None, "replica", "tensor"),
            P(None, "replica", "tensor"),
            P("replica", None, "tensor"),
            P("replica", None, "tensor"),
            P("replica", "tensor", None),
            P("replica"),
            P(),
        ),
        out_specs=(
            P("replica", None, "tensor"),
            P("replica", None, "tensor"),
            P("replica", "tensor", None),
            P(None, "replica", "tensor"),
        ),
        check_vma=False,
    )
```

```python
from functools import partial

import jax
import jax.numpy as jnp
from jax import lax
from jax.experimental import pallas as pl
from jax.experimental.pallas import tpu as pltpu
from jax.sharding import PartitionSpec as P

Y, XH = 4, 2
BF16, F32 = jnp.bfloat16, jnp.float32
ANY = pl.BlockSpec(memory_space=pl.ANY)
VMEM = pl.BlockSpec(memory_space=pltpu.VMEM)
SMEM = pl.BlockSpec(memory_space=pltpu.SMEM)


def tensor_permute(value, move):
    pairs = []
    for y in range(Y):
        for xh in range(XH):
            to_y, to_xh = move(y, xh)
            pairs.append((y * XH + xh, to_y % Y * XH + to_xh % XH))
    return lax.ppermute(value, "tensor", pairs)


def flip_x(value):
    return tensor_permute(value, lambda y, xh: (y, xh + 1))


def shift_y(value, by):
    return tensor_permute(value, lambda y, xh: (y + by, xh))


def flip_y(value, low):
    return tensor_permute(value, lambda y, xh: (y ^ 1 if low else 3 - y, xh))


def place(me, dy, dxh):
    return ((me + dy * XH) & (Y * XH - XH)) | ((me + dxh) & (XH - 1))


def gather(own):
    below = shift_y(own, 1)
    above = shift_y(own, -1)
    other = flip_x(own)
    far = shift_y(own, 2)
    other, below, above = lax.optimization_barrier((other, below, above))
    return [own, other, below, above, shift_y(other, 1), shift_y(other, -1), far, flip_x(far)]


def gather_near(own):
    return [flip_x(own), shift_y(own, 1), shift_y(own, -1), shift_y(own, 2)]


def gather_across(own, near):
    other, below, above, far = near
    return [own, other, below, above, far, flip_x(jnp.stack([below, above, far]))]


PIECES = [(0, 0), (0, 1), (-1, 0), (1, 0), (-1, 1), (1, 1), (2, 0), (2, 1)]


def fetch(me, pieces, first, out, sems):
    rows = out.shape[0]
    width = out.shape[1] // (Y * XH)
    copies = []
    for number, (piece, (dy, dxh)) in enumerate(zip(pieces, PIECES)):
        at = pl.multiple_of(place(me, dy, dxh) * width, width)
        copies.append(
            pltpu.make_async_copy(
                piece.at[pl.ds(first, rows)], out.at[:, pl.ds(at, width)], sems.at[number]
            )
        )
    for copy in copies:
        copy.start()
    return copies


def contract(a, b, dim_a, dim_b):
    return lax.dot_general(
        a, b, (((dim_a,), (dim_b,)), ((), ())), preferred_element_type=F32
    )


def step_kernel(second, *refs):
    if second:
        own, flipped, below, above, far, across, *refs = refs
        pieces = [own, flipped, below, above, across.at[0], across.at[1], far, across.at[2]]
    else:
        pieces, refs = refs[:8], refs[8:]
    sources, refs = refs[:3], refs[3:]
    weights, grads, hidden, squares_out, *refs = refs
    x, dy, gates, ups, d_gate, d_up, x_sems, dy_sems, w_sems = refs
    tokens, features = x.shape
    me = lax.axis_index("tensor")

    def load(number):
        copy = pltpu.make_async_copy(sources[number], weights.at[number], w_sems.at[number])
        copy.start()
        return copy

    loads = [load(0)]
    x_copies = fetch(me, pieces, 0, x, x_sems)
    loads += [load(1), load(2)]
    dy_copies = fetch(me, pieces, tokens, dy, dy_sems)

    chunk = 256
    wide = 512

    def over_tokens(body):
        def step(block, _):
            body(pl.ds(pl.multiple_of(block * chunk, chunk), chunk))
            return 0

        lax.fori_loop(0, tokens // chunk, step, 0)

    def gate_pass(at):
        gates[:, at] = contract(weights[0], x[at], 1, 1)

    def up_pass(at):
        up = contract(weights[1], x[at], 1, 1)
        gate = gates[:, at]
        ups[:, at] = up
        hidden[:, at] = (gate * jax.nn.sigmoid(gate) * up).astype(BF16)

    def back_pass(at):
        back = contract(weights[2], dy[at], 1, 1)
        gate = gates[:, at]
        sigma = jax.nn.sigmoid(gate)
        d_gate[:, at] = (
            back * ups[:, at] * sigma * (1.0 + gate * (1.0 - sigma))
        ).astype(BF16)
        d_up[:, at] = (back * (gate * sigma)).astype(BF16)

    loads[0].wait()
    for copy in x_copies:
        copy.wait()
    over_tokens(gate_pass)
    loads[1].wait()
    over_tokens(up_pass)
    loads[2].wait()
    for copy in dy_copies:
        copy.wait()
    over_tokens(back_pass)

    def columns(block, total):
        at = pl.ds(pl.multiple_of(block * wide, wide), wide)
        for number, (left, right) in enumerate([(d_gate, x), (d_up, x), (hidden, dy)]):
            grad = contract(left[...], right[:, at], 1, 0)
            grads[number, :, at] = grad.astype(BF16)
            total = total + jnp.sum(grad * grad, axis=0, keepdims=True)
        return total

    blocks = features // wide
    total = lax.fori_loop(0, blocks, columns, jnp.zeros((1, wide), F32))
    squares_out[...] = jnp.broadcast_to(jnp.sum(total, axis=1, keepdims=True), (8, 128))


def step_pass(pieces, weights, second):
    rows, width = pieces[0].shape
    tokens = rows // 2
    features = width * Y * XH
    units = weights[0].shape[-2]
    size = tokens * features * units
    stack = (3, units, features)
    return pl.pallas_call(
        partial(step_kernel, second),
        out_shape=[
            pltpu.VMEM(stack, BF16),
            pltpu.VMEM(stack, BF16),
            jax.ShapeDtypeStruct((units, tokens), BF16),
            jax.ShapeDtypeStruct((8, 128), F32),
        ],
        in_specs=[ANY] * (len(pieces) + len(weights)),
        out_specs=[VMEM] * 4,
        scratch_shapes=[
            pltpu.VMEM((tokens, features), BF16),
            pltpu.VMEM((tokens, features), BF16),
            pltpu.VMEM((units, tokens), F32),
            pltpu.VMEM((units, tokens), F32),
            pltpu.VMEM((units, tokens), BF16),
            pltpu.VMEM((units, tokens), BF16),
            pltpu.SemaphoreType.DMA((8,)),
            pltpu.SemaphoreType.DMA((8,)),
            pltpu.SemaphoreType.DMA((3,)),
        ],
        name="step",
        compiler_params=pltpu.CompilerParams(vmem_limit_bytes=28 << 20),
        cost_estimate=pl.CostEstimate(
            flops=12 * size, bytes_accessed=16 << 20, transcendentals=2 * units * tokens
        ),
    )(*pieces, *weights)


def update_kernel(rate, squares, stack, grads, both, down):
    scale = rate[0] / jnp.sqrt(squares[0:1, 0:1] + 1e-06)

    def rows(block, _):
        at = pl.ds(pl.multiple_of(block * 32, 32), 32)
        for number in range(3):
            own, grad = stack[number, at].astype(F32), grads[number, at].astype(F32)
            to = both.at[number] if number < 2 else down
            to[at] = (own - scale * grad).astype(BF16)
        return 0

    lax.fori_loop(0, stack.shape[1] // 32, rows, 0)


def updated(rates, squares, stack, grads):
    return pl.pallas_call(
        update_kernel,
        out_shape=[pltpu.VMEM((2, *stack.shape[1:]), BF16), pltpu.VMEM(stack.shape[1:], BF16)],
        in_specs=[SMEM, VMEM, VMEM, VMEM],
        out_specs=[VMEM, VMEM],
        name="update",
        compiler_params=pltpu.CompilerParams(vmem_limit_bytes=18 << 20),
        cost_estimate=pl.CostEstimate(
            flops=2 * stack.size, bytes_accessed=6 * stack.size, transcendentals=0
        ),
    )(rates, squares, stack, grads)


def outputs_kernel(hidden1, hidden2, down1, stack2, kept, sent, passed, hidden, down, sems):
    me = lax.axis_index("tensor")
    pairs = [(hidden1, hidden.at[0]), (hidden2, hidden.at[1])]
    pairs += [(down1, down.at[0]), (stack2.at[2], down.at[1])]
    loads = [
        pltpu.make_async_copy(source, to, sems.at[number])
        for number, (source, to) in enumerate(pairs)
    ]
    for load in loads:
        load.start()
    for load in loads:
        load.wait()
    tokens = hidden.shape[2]
    width = kept.shape[2]
    y, xh = me // XH, me % XH

    def part(index, _):
        number, dxh = index // 2, index % 2
        rows = pl.ds(pl.multiple_of(number * tokens, tokens), tokens)
        outs = [
            (kept.at[dxh], y),
            (sent.at[0, dxh], y ^ 1),
            (sent.at[1, dxh], 3 - (y ^ 1)),
            (passed.at[dxh], 3 - y),
        ]
        for out, to in outs:
            place = (to * XH + (xh ^ dxh)) * width
            at = pl.ds(pl.multiple_of(place, width), width)
            out[rows] = contract(hidden[number], down[number, :, at], 0, 0).astype(BF16)
        return 0

    lax.fori_loop(0, 4, part, 0)


def outputs(hidden1, hidden2, down1, stack2):
    units, tokens = hidden1.shape
    features = down1.shape[1]
    block = (2, 2 * tokens, features // (Y * XH))
    return pl.pallas_call(
        outputs_kernel,
        out_shape=[
            jax.ShapeDtypeStruct(block, BF16),
            jax.ShapeDtypeStruct((2, *block), BF16),
            jax.ShapeDtypeStruct(block, BF16),
        ],
        in_specs=[ANY] * 4,
        out_specs=[VMEM] * 3,
        scratch_shapes=[
            pltpu.VMEM((2, units, tokens), BF16),
            pltpu.VMEM((2, units, features), BF16),
            pltpu.SemaphoreType.DMA((4,)),
        ],
        name="outputs",
        compiler_params=pltpu.CompilerParams(vmem_limit_bytes=20 << 20),
        cost_estimate=pl.CostEstimate(
            flops=4 * tokens * features * units, bytes_accessed=8 << 20, transcendentals=0
        ),
    )(hidden1, hidden2, down1, stack2)


def add_kernel(picks, *refs):
    *parts, out = refs
    shape = out.shape[:-2]

    def rows(block, _):
        at = pl.ds(pl.multiple_of(block * 32, 32), 32)
        for index in range(shape[0] if shape else 1):
            lead = (index,) if shape else ()
            total = sum(part[(*pick, *lead, at)].astype(F32) for part, pick in zip(parts, picks))
            out[(*lead, at)] = total.astype(out.dtype)
        return 0

    lax.fori_loop(0, out.shape[-2] // 32, rows, 0)


def add(*parts):
    arrays, picks = zip(*parts)
    shape = arrays[0].shape[len(picks[0]) :]
    return pl.pallas_call(
        partial(add_kernel, picks),
        out_shape=jax.ShapeDtypeStruct(shape, BF16),
        in_specs=[VMEM] * len(arrays),
        out_specs=VMEM,
        name="add",
        compiler_params=pltpu.CompilerParams(vmem_limit_bytes=20 << 20),
        cost_estimate=pl.CostEstimate(flops=1 << 20, bytes_accessed=4 << 20, transcendentals=0),
    )(*arrays)


def scatter_sum(kept, sent, passed):
    came = flip_y(sent, True)
    last = flip_y(add((passed, ()), (came, (1,))), False)
    across = flip_x(add((kept, (1,)), (came, (0, 1)), (last, (1,))))
    return add((kept, (0,)), (came, (0, 0)), (last, (0,)), (across, ()))


def group_sum(value):
    near = value + flip_x(value)
    value = near + flip_y(near, True)
    value = value + flip_y(value, False)
    return value, near


def swap(value, number):
    pairs = [(source, source ^ 2**number) for source in range(lax.axis_size("replica"))]
    return lax.ppermute(value, "replica", pairs)


def mean_kernel(fresh, other, *refs):
    *outs, theirs, in_sems, out_sems = refs
    count, rows = len(outs), outs[0].shape[0]
    half = rows // 2
    blocks = [(part, pl.ds(first, half)) for part in range(count) for first in (0, half)]

    def copy(number, out):
        part, at = blocks[number]
        if out:
            return pltpu.make_async_copy(
                theirs.at[part, at], outs[part].at[at], out_sems.at[number]
            )
        source = other.at[part, at] if count > 1 else other.at[at]
        return pltpu.make_async_copy(source, theirs.at[part, at], in_sems.at[number])

    for number in range(len(blocks)):
        copy(number, False).start()
    for number, (part, at) in enumerate(blocks):
        copy(number, False).wait()

        def some(index, _):
            at = pl.ds(pl.multiple_of((number % 2) * half + index * 16, 16), 16)
            own = fresh[part, at] if count > 1 else fresh[at]
            total = own.astype(F32) + theirs[part, at].astype(F32)
            theirs[part, at] = (total * 0.5).astype(BF16)
            return 0

        lax.fori_loop(0, half // 16, some, 0)
        copy(number, True).start()
    for number in range(len(blocks)):
        copy(number, True).wait()


def mean(fresh, other):
    count = fresh.shape[0] if fresh.ndim == 3 else 1
    shape = fresh.shape[-2:]
    return pl.pallas_call(
        mean_kernel,
        out_shape=[pltpu.HBM(shape, BF16)] * count,
        in_specs=[VMEM, ANY],
        out_specs=[ANY] * count,
        scratch_shapes=[
            pltpu.VMEM((count, *shape), BF16),
            pltpu.SemaphoreType.DMA((2 * count,)),
            pltpu.SemaphoreType.DMA((2 * count,)),
        ],
        name="mean",
        compiler_params=pltpu.CompilerParams(vmem_limit_bytes=10 << 20),
        cost_estimate=pl.CostEstimate(
            flops=2 * fresh.size, bytes_accessed=6 * fresh.size, transcendentals=0
        ),
    )(fresh, other)


def mix(number, both, down):
    others = swap(both, number), swap(down, number)
    first = mean(both, others[0])
    return first + mean(down, after(others[1], first[0]))


def mix_last(number, both, down, *blocks):
    return mix(number, both, down), scatter_sum(*blocks)


def by_bit(bit, handler, *values):
    return lax.switch(bit, [partial(handler, number) for number in range(4)], *values)


def after(value, *others):
    return lax.optimization_barrier((value, *others))[0]


def local(inputs, out_grads, gate_weight, up_weight, down_weight, rates, partner_bits):
    weights = [gate_weight[0].T, up_weight[0].T, down_weight[0]]
    own1 = jnp.concatenate([inputs[0], out_grads[0]])
    pieces1 = gather(own1)
    own2 = jnp.concatenate([inputs[1], out_grads[1]])
    own2 = after(own2, pieces1[4], pieces1[5], pieces1[6])
    near2 = gather_near(own2)

    stack, grads, hidden1, squares = step_pass(pieces1, weights, False)
    squares, flipped = group_sum(squares)
    near2 = list(lax.optimization_barrier((*near2, flipped))[:4])
    pieces2 = gather_across(own2, near2)
    pieces2 = [pltpu.with_memory_space_constraint(piece, pltpu.HBM) for piece in pieces2]
    fresh = updated(rates, squares, stack, grads)
    middle = by_bit(partner_bits[0], mix, *fresh)

    stack, grads, hidden2, squares = step_pass(pieces2, middle, True)
    squares, _ = group_sum(squares)
    blocks = outputs(hidden1, hidden2, weights[2], stack)
    fresh = updated(rates, squares, stack, grads)
    new, results = by_bit(partner_bits[1], mix_last, *fresh, *blocks)
    return (new[0].T[None], new[1].T[None], new[2][None], results.reshape(inputs.shape))


def solution(mesh):
    return jax.shard_map(
        local,
        mesh=mesh,
        in_specs=(
            P(None, "replica", "tensor"),
            P(None, "replica", "tensor"),
            P("replica", None, "tensor"),
            P("replica", None, "tensor"),
            P("replica", "tensor", None),
            P("replica"),
            P(),
        ),
        out_specs=(
            P("replica", None, "tensor"),
            P("replica", None, "tensor"),
            P("replica", "tensor", None),
            P(None, "replica", "tensor"),
        ),
        check_vma=False,
    )
```

```python
from functools import partial

import jax
import jax.numpy as jnp
from jax import lax
from jax.experimental import pallas as pl
from jax.experimental.pallas import tpu as pltpu
from jax.sharding import PartitionSpec as P

Y, XH = 4, 2
BF16, F32 = jnp.bfloat16, jnp.float32
ANY = pl.BlockSpec(memory_space=pl.ANY)
VMEM = pl.BlockSpec(memory_space=pltpu.VMEM)
SMEM = pl.BlockSpec(memory_space=pltpu.SMEM)


def tensor_permute(value, move):
    pairs = []
    for y in range(Y):
        for xh in range(XH):
            to_y, to_xh = move(y, xh)
            pairs.append((y * XH + xh, to_y % Y * XH + to_xh % XH))
    return lax.ppermute(value, "tensor", pairs)


def flip_x(value):
    return tensor_permute(value, lambda y, xh: (y, xh + 1))


def shift_y(value, by):
    return tensor_permute(value, lambda y, xh: (y + by, xh))


def flip_y(value, low):
    return tensor_permute(value, lambda y, xh: (y ^ 1 if low else 3 - y, xh))


def place(me, dy, dxh):
    return ((me + dy * XH) & (Y * XH - XH)) | ((me + dxh) & (XH - 1))


def gather(own):
    below = shift_y(own, 1)
    above = shift_y(own, -1)
    other = flip_x(own)
    far = shift_y(own, 2)
    other, below, above = lax.optimization_barrier((other, below, above))
    return [own, other, below, above, shift_y(other, 1), shift_y(other, -1), far, flip_x(far)]


def gather_near(own):
    return [flip_x(own), shift_y(own, 1), shift_y(own, -1), shift_y(own, 2)]


def gather_across(own, near):
    other, below, above, far = near
    return [own, other, below, above, far, flip_x(jnp.stack([below, above, far]))]


PIECES = [(0, 0), (0, 1), (-1, 0), (1, 0), (-1, 1), (1, 1), (2, 0), (2, 1)]


def fetch(me, pieces, first, out, sems):
    rows = out.shape[0]
    width = out.shape[1] // (Y * XH)
    copies = []
    for number, (piece, (dy, dxh)) in enumerate(zip(pieces, PIECES)):
        at = pl.multiple_of(place(me, dy, dxh) * width, width)
        copies.append(
            pltpu.make_async_copy(
                piece.at[pl.ds(first, rows)], out.at[:, pl.ds(at, width)], sems.at[number]
            )
        )
    for copy in copies:
        copy.start()
    return copies


def contract(a, b, dim_a, dim_b):
    return lax.dot_general(
        a, b, (((dim_a,), (dim_b,)), ((), ())), preferred_element_type=F32
    )


def step_kernel(second, *refs):
    if second:
        own, flipped, below, above, far, across, *refs = refs
        pieces = [own, flipped, below, above, across.at[0], across.at[1], far, across.at[2]]
    else:
        pieces, refs = refs[:8], refs[8:]
    sources, refs = refs[:3], refs[3:]
    weights, grads, hidden, squares_out, *refs = refs
    x, dy, gates, ups, d_gate, d_up, x_sems, dy_sems, w_sems = refs
    tokens, features = x.shape
    me = lax.axis_index("tensor")

    def load(number):
        copy = pltpu.make_async_copy(sources[number], weights.at[number], w_sems.at[number])
        copy.start()
        return copy

    loads = [load(0)]
    x_copies = fetch(me, pieces, 0, x, x_sems)
    loads += [load(1), load(2)]
    dy_copies = fetch(me, pieces, tokens, dy, dy_sems)

    chunk = 256
    wide = 512

    def over_tokens(body):
        def step(block, _):
            body(pl.ds(pl.multiple_of(block * chunk, chunk), chunk))
            return 0

        lax.fori_loop(0, tokens // chunk, step, 0)

    def gate_pass(at):
        gates[:, at] = contract(weights[0], x[at], 1, 1)

    def up_pass(at):
        up = contract(weights[1], x[at], 1, 1)
        gate = gates[:, at]
        ups[:, at] = up
        hidden[:, at] = (gate * jax.nn.sigmoid(gate) * up).astype(BF16)

    def back_pass(at):
        back = contract(weights[2], dy[at], 1, 1)
        gate = gates[:, at]
        sigma = jax.nn.sigmoid(gate)
        d_gate[:, at] = (
            back * ups[:, at] * sigma * (1.0 + gate * (1.0 - sigma))
        ).astype(BF16)
        d_up[:, at] = (back * (gate * sigma)).astype(BF16)

    loads[0].wait()
    for copy in x_copies:
        copy.wait()
    over_tokens(gate_pass)
    loads[1].wait()
    over_tokens(up_pass)
    loads[2].wait()
    for copy in dy_copies:
        copy.wait()
    over_tokens(back_pass)

    def columns(block, total):
        at = pl.ds(pl.multiple_of(block * wide, wide), wide)
        for number, (left, right) in enumerate([(d_gate, x), (d_up, x), (hidden, dy)]):
            grad = contract(left[...], right[:, at], 1, 0)
            grads[number, :, at] = grad.astype(BF16)
            total = total + jnp.sum(grad * grad, axis=0, keepdims=True)
        return total

    blocks = features // wide
    total = lax.fori_loop(0, blocks, columns, jnp.zeros((1, wide), F32))
    squares_out[...] = jnp.broadcast_to(jnp.sum(total, axis=1, keepdims=True), (8, 128))


def step_pass(pieces, weights, second):
    rows, width = pieces[0].shape
    tokens = rows // 2
    features = width * Y * XH
    units = weights[0].shape[-2]
    size = tokens * features * units
    stack = (3, units, features)
    return pl.pallas_call(
        partial(step_kernel, second),
        out_shape=[
            pltpu.VMEM(stack, BF16),
            pltpu.VMEM(stack, BF16),
            jax.ShapeDtypeStruct((units, tokens), BF16),
            jax.ShapeDtypeStruct((8, 128), F32),
        ],
        in_specs=[ANY] * (len(pieces) + len(weights)),
        out_specs=[VMEM] * 4,
        scratch_shapes=[
            pltpu.VMEM((tokens, features), BF16),
            pltpu.VMEM((tokens, features), BF16),
            pltpu.VMEM((units, tokens), F32),
            pltpu.VMEM((units, tokens), F32),
            pltpu.VMEM((units, tokens), BF16),
            pltpu.VMEM((units, tokens), BF16),
            pltpu.SemaphoreType.DMA((8,)),
            pltpu.SemaphoreType.DMA((8,)),
            pltpu.SemaphoreType.DMA((3,)),
        ],
        name="step",
        compiler_params=pltpu.CompilerParams(vmem_limit_bytes=28 << 20),
        cost_estimate=pl.CostEstimate(
            flops=12 * size, bytes_accessed=16 << 20, transcendentals=2 * units * tokens
        ),
    )(*pieces, *weights)


def update_kernel(rate, squares, stack, grads, both, down):
    scale = rate[0] / jnp.sqrt(squares[0:1, 0:1] + 1e-06)

    def rows(block, _):
        at = pl.ds(pl.multiple_of(block * 32, 32), 32)
        for number in range(3):
            own, grad = stack[number, at].astype(F32), grads[number, at].astype(F32)
            to = both.at[number] if number < 2 else down
            to[at] = (own - scale * grad).astype(BF16)
        return 0

    lax.fori_loop(0, stack.shape[1] // 32, rows, 0)


def updated(rates, squares, stack, grads):
    return pl.pallas_call(
        update_kernel,
        out_shape=[pltpu.VMEM((2, *stack.shape[1:]), BF16), pltpu.VMEM(stack.shape[1:], BF16)],
        in_specs=[SMEM, VMEM, VMEM, VMEM],
        out_specs=[VMEM, VMEM],
        name="update",
        compiler_params=pltpu.CompilerParams(vmem_limit_bytes=18 << 20),
        cost_estimate=pl.CostEstimate(
            flops=2 * stack.size, bytes_accessed=6 * stack.size, transcendentals=0
        ),
    )(rates, squares, stack, grads)


def outputs_kernel(hidden1, hidden2, down1, stack2, kept, sent, passed, hidden, down, sems):
    me = lax.axis_index("tensor")
    pairs = [(hidden1, hidden.at[0]), (hidden2, hidden.at[1])]
    pairs += [(down1, down.at[0]), (stack2.at[2], down.at[1])]
    loads = [
        pltpu.make_async_copy(source, to, sems.at[number])
        for number, (source, to) in enumerate(pairs)
    ]
    for load in loads:
        load.start()
    for load in loads:
        load.wait()
    tokens = hidden.shape[2]
    width = kept.shape[2]
    y, xh = me // XH, me % XH

    def part(index, _):
        number, dxh = index // 2, index % 2
        rows = pl.ds(pl.multiple_of(number * tokens, tokens), tokens)
        outs = [
            (kept.at[dxh], y),
            (sent.at[0, dxh], y ^ 1),
            (sent.at[1, dxh], 3 - (y ^ 1)),
            (passed.at[dxh], 3 - y),
        ]
        for out, to in outs:
            place = (to * XH + (xh ^ dxh)) * width
            at = pl.ds(pl.multiple_of(place, width), width)
            out[rows] = contract(hidden[number], down[number, :, at], 0, 0).astype(BF16)
        return 0

    lax.fori_loop(0, 4, part, 0)


def outputs(hidden1, hidden2, down1, stack2):
    units, tokens = hidden1.shape
    features = down1.shape[1]
    block = (2, 2 * tokens, features // (Y * XH))
    return pl.pallas_call(
        outputs_kernel,
        out_shape=[
            jax.ShapeDtypeStruct(block, BF16),
            jax.ShapeDtypeStruct((2, *block), BF16),
            jax.ShapeDtypeStruct(block, BF16),
        ],
        in_specs=[ANY] * 4,
        out_specs=[VMEM] * 3,
        scratch_shapes=[
            pltpu.VMEM((2, units, tokens), BF16),
            pltpu.VMEM((2, units, features), BF16),
            pltpu.SemaphoreType.DMA((4,)),
        ],
        name="outputs",
        compiler_params=pltpu.CompilerParams(vmem_limit_bytes=20 << 20),
        cost_estimate=pl.CostEstimate(
            flops=4 * tokens * features * units, bytes_accessed=8 << 20, transcendentals=0
        ),
    )(hidden1, hidden2, down1, stack2)


def add_kernel(picks, *refs):
    *parts, out = refs
    shape = out.shape[:-2]

    def rows(block, _):
        at = pl.ds(pl.multiple_of(block * 32, 32), 32)
        for index in range(shape[0] if shape else 1):
            lead = (index,) if shape else ()
            total = sum(part[(*pick, *lead, at)].astype(F32) for part, pick in zip(parts, picks))
            out[(*lead, at)] = total.astype(out.dtype)
        return 0

    lax.fori_loop(0, out.shape[-2] // 32, rows, 0)


def add(*parts):
    arrays, picks = zip(*parts)
    shape = arrays[0].shape[len(picks[0]) :]
    return pl.pallas_call(
        partial(add_kernel, picks),
        out_shape=jax.ShapeDtypeStruct(shape, BF16),
        in_specs=[VMEM] * len(arrays),
        out_specs=VMEM,
        name="add",
        compiler_params=pltpu.CompilerParams(vmem_limit_bytes=20 << 20),
        cost_estimate=pl.CostEstimate(flops=1 << 20, bytes_accessed=4 << 20, transcendentals=0),
    )(*arrays)


def scatter_sum(kept, sent, passed):
    came = flip_y(sent, True)
    last = flip_y(add((passed, ()), (came, (1,))), False)
    across = flip_x(add((kept, (1,)), (came, (0, 1)), (last, (1,))))
    return add((kept, (0,)), (came, (0, 0)), (last, (0,)), (across, ()))


def scatter_sum_direct(kept, sent, passed, first):
    came = [flip_y(sent[0], True), flip_y(passed, False), shift_y(sent[1], 2)]
    came = lax.optimization_barrier((*came, *first))[:3]
    across = flip_x(add((kept, (1,)), *((part, (1,)) for part in came)))
    return add((kept, (0,)), *((part, (0,)) for part in came), (across, ()))


def group_sum(value):
    value = value + flip_x(value)
    value = value + flip_y(value, True)
    return value + flip_y(value, False)


def swap(value, number):
    pairs = [(source, source ^ 2**number) for source in range(lax.axis_size("replica"))]
    return lax.ppermute(value, "replica", pairs)


def mean_kernel(fresh, other, *refs):
    *outs, theirs, in_sems, out_sems = refs
    count, rows = len(outs), outs[0].shape[0]
    half = rows // 2
    blocks = [(part, pl.ds(first, half)) for part in range(count) for first in (0, half)]

    def copy(number, out):
        part, at = blocks[number]
        if out:
            return pltpu.make_async_copy(
                theirs.at[part, at], outs[part].at[at], out_sems.at[number]
            )
        source = other.at[part, at] if count > 1 else other.at[at]
        return pltpu.make_async_copy(source, theirs.at[part, at], in_sems.at[number])

    for number in range(len(blocks)):
        copy(number, False).start()
    for number, (part, at) in enumerate(blocks):
        copy(number, False).wait()

        def some(index, _):
            at = pl.ds(pl.multiple_of((number % 2) * half + index * 16, 16), 16)
            own = fresh[part, at] if count > 1 else fresh[at]
            total = own.astype(F32) + theirs[part, at].astype(F32)
            theirs[part, at] = (total * 0.5).astype(BF16)
            return 0

        lax.fori_loop(0, half // 16, some, 0)
        copy(number, True).start()
    for number in range(len(blocks)):
        copy(number, True).wait()


def mean(fresh, other):
    count = fresh.shape[0] if fresh.ndim == 3 else 1
    shape = fresh.shape[-2:]
    return pl.pallas_call(
        mean_kernel,
        out_shape=[pltpu.HBM(shape, BF16)] * count,
        in_specs=[VMEM, ANY],
        out_specs=[ANY] * count,
        scratch_shapes=[
            pltpu.VMEM((count, *shape), BF16),
            pltpu.SemaphoreType.DMA((2 * count,)),
            pltpu.SemaphoreType.DMA((2 * count,)),
        ],
        name="mean",
        compiler_params=pltpu.CompilerParams(vmem_limit_bytes=10 << 20),
        cost_estimate=pl.CostEstimate(
            flops=2 * fresh.size, bytes_accessed=6 * fresh.size, transcendentals=0
        ),
    )(fresh, other)


def mix(number, both, down):
    others = swap(both, number), swap(down, number)
    first = mean(both, others[0])
    return first + mean(down, after(others[1], first[0]))


def mix_last(number, both, down, *blocks):
    new = mix(number, both, down)
    if number == 0:
        return new, scatter_sum_direct(*blocks, new)
    return new, scatter_sum(*blocks)


def by_bit(bit, handler, *values):
    return lax.switch(bit, [partial(handler, number) for number in range(4)], *values)


def after(value, *others):
    return lax.optimization_barrier((value, *others))[0]


def local(inputs, out_grads, gate_weight, up_weight, down_weight, rates, partner_bits):
    weights = [gate_weight[0].T, up_weight[0].T, down_weight[0]]
    weights[1] = pltpu.with_memory_space_constraint(weights[1], pltpu.HBM)
    own1 = jnp.concatenate([inputs[0], out_grads[0]])
    pieces1 = gather(own1)
    later = lax.optimization_barrier((inputs, out_grads, *pieces1[4:7]))
    own2 = jnp.concatenate([later[0][1], later[1][1]])
    near2 = gather_near(own2)

    stack, grads, hidden1, squares = step_pass(pieces1, weights, False)
    squares = group_sum(squares)
    near2 = list(lax.optimization_barrier((*near2, squares))[:4])
    pieces2 = gather_across(own2, near2)
    pieces2 = [pltpu.with_memory_space_constraint(piece, pltpu.HBM) for piece in pieces2]
    fresh = updated(rates, squares, stack, grads)
    middle = by_bit(partner_bits[0], mix, *fresh)

    stack, grads, hidden2, squares = step_pass(pieces2, middle, True)
    squares = group_sum(squares)
    blocks = outputs(hidden1, hidden2, weights[2], stack)
    fresh = updated(rates, squares, stack, grads)
    new, results = by_bit(partner_bits[1], mix_last, *fresh, *blocks)
    return (new[0].T[None], new[1].T[None], new[2][None], results.reshape(inputs.shape))


def solution(mesh):
    return jax.shard_map(
        local,
        mesh=mesh,
        in_specs=(
            P(None, "replica", "tensor"),
            P(None, "replica", "tensor"),
            P("replica", None, "tensor"),
            P("replica", None, "tensor"),
            P("replica", "tensor", None),
            P("replica"),
            P(),
        ),
        out_specs=(
            P("replica", None, "tensor"),
            P("replica", None, "tensor"),
            P("replica", "tensor", None),
            P(None, "replica", "tensor"),
        ),
        check_vma=False,
    )
```

```python
from functools import partial

import jax
import jax.numpy as jnp
from jax import lax
from jax.experimental import pallas as pl
from jax.experimental.pallas import tpu as pltpu
from jax.sharding import PartitionSpec as P


Y, XH = 4, 2
BF16, F32 = jnp.bfloat16, jnp.float32
ANY = pl.BlockSpec(memory_space=pl.ANY)
VMEM = pl.BlockSpec(memory_space=pltpu.VMEM)
SMEM = pl.BlockSpec(memory_space=pltpu.SMEM)


def tensor_permute(value, move):
    pairs = []
    for y in range(Y):
        for xh in range(XH):
            to_y, to_xh = move(y, xh)
            pairs.append((y * XH + xh, to_y % Y * XH + to_xh % XH))
    return lax.ppermute(value, "tensor", pairs)


def flip_x(value):
    return tensor_permute(value, lambda y, xh: (y, xh + 1))


def shift_y(value, by):
    return tensor_permute(value, lambda y, xh: (y + by, xh))


def flip_y(value, low):
    return tensor_permute(value, lambda y, xh: (y ^ 1 if low else 3 - y, xh))


def place(me, dy, dxh):
    return ((me + dy * XH) & (Y * XH - XH)) | ((me + dxh) & (XH - 1))


def gather(own):
    below = shift_y(own, 1)
    above = shift_y(own, -1)
    other = flip_x(own)
    far = shift_y(own, 2)
    other, below, above = lax.optimization_barrier((other, below, above))
    return [own, other, below, above, shift_y(other, 1), shift_y(other, -1), far, flip_x(far)]


def gather_near(own):
    return [flip_x(own), shift_y(own, 1), shift_y(own, -1), shift_y(own, 2)]


def gather_across(own, near):
    other, below, above, far = near
    theirs = jnp.stack([below, above, far])
    theirs = flip_x(theirs)
    return [own, other, below, above, far, theirs]


PIECES = [(0, 0), (0, 1), (-1, 0), (1, 0), (-1, 1), (1, 1), (2, 0), (2, 1)]


def fetch(me, pieces, first, out, sems):
    rows = out.shape[0]
    width = out.shape[1] // (Y * XH)
    copies = []
    for number, (piece, (dy, dxh)) in enumerate(zip(pieces, PIECES)):
        at = pl.multiple_of(place(me, dy, dxh) * width, width)
        copies.append(
            pltpu.make_async_copy(
                piece.at[pl.ds(first, rows)], out.at[:, pl.ds(at, width)], sems.at[number]
            )
        )
    for copy in copies:
        copy.start()
    return copies


def contract(a, b, dim_a, dim_b):
    return lax.dot_general(
        a, b, (((dim_a,), (dim_b,)), ((), ())), preferred_element_type=F32
    )


def step_kernel(second, *refs):
    if second:
        own, flipped, below, above, far, across, *refs = refs
        pieces = [own, flipped, below, above, across.at[0], across.at[1], far, across.at[2]]
    else:
        pieces, refs = refs[:8], refs[8:]
    sources, refs = refs[:3], refs[3:]
    weights, grads, hidden, squares_out, *refs = refs
    x, dy, gates, ups, d_gate, d_up, x_sems, dy_sems, w_sems = refs
    tokens, features = x.shape
    me = lax.axis_index("tensor")

    def load(number):
        copy = pltpu.make_async_copy(sources[number], weights.at[number], w_sems.at[number])
        copy.start()
        return copy

    loads = [load(0)]
    x_copies = fetch(me, pieces, 0, x, x_sems)
    loads += [load(1), load(2)]
    dy_copies = fetch(me, pieces, tokens, dy, dy_sems)

    chunk = 256
    wide = 512

    def over_tokens(body):
        def step(block, _):
            body(pl.ds(pl.multiple_of(block * chunk, chunk), chunk))
            return 0

        lax.fori_loop(0, tokens // chunk, step, 0)

    def gate_pass(at):
        gates[:, at] = contract(weights[0], x[at], 1, 1)

    def up_pass(at):
        up = contract(weights[1], x[at], 1, 1)
        gate = gates[:, at]
        ups[:, at] = up
        hidden[:, at] = (gate * jax.nn.sigmoid(gate) * up).astype(BF16)

    def back_pass(at):
        back = contract(weights[2], dy[at], 1, 1)
        gate = gates[:, at]
        sigma = jax.nn.sigmoid(gate)
        d_gate[:, at] = (
            back * ups[:, at] * sigma * (1.0 + gate * (1.0 - sigma))
        ).astype(BF16)
        d_up[:, at] = (back * (gate * sigma)).astype(BF16)

    loads[0].wait()
    for copy in x_copies:
        copy.wait()
    over_tokens(gate_pass)
    loads[1].wait()
    over_tokens(up_pass)
    loads[2].wait()
    for copy in dy_copies:
        copy.wait()
    over_tokens(back_pass)

    def columns(block, total):
        at = pl.ds(pl.multiple_of(block * wide, wide), wide)
        for number, (left, right) in enumerate([(d_gate, x), (d_up, x), (hidden, dy)]):
            grad = contract(left[...], right[:, at], 1, 0)
            grads[number, :, at] = grad.astype(BF16)
            total = total + jnp.sum(grad * grad, axis=0, keepdims=True)
        return total

    blocks = features // wide
    total = lax.fori_loop(0, blocks, columns, jnp.zeros((1, wide), F32))
    squares_out[...] = jnp.broadcast_to(jnp.sum(total, axis=1, keepdims=True), (8, 128))


def step_pass(pieces, weights, second):
    rows, width = pieces[0].shape
    tokens = rows // 2
    features = width * Y * XH
    units = weights[0].shape[-2]
    size = tokens * features * units
    stack = (3, units, features)
    return pl.pallas_call(
        partial(step_kernel, second),
        out_shape=[
            pltpu.VMEM(stack, BF16),
            pltpu.VMEM(stack, BF16),
            jax.ShapeDtypeStruct((units, tokens), BF16),
            jax.ShapeDtypeStruct((8, 128), F32),
        ],
        in_specs=[ANY] * (len(pieces) + len(weights)),
        out_specs=[VMEM] * 4,
        scratch_shapes=[
            pltpu.VMEM((tokens, features), BF16),
            pltpu.VMEM((tokens, features), BF16),
            pltpu.VMEM((units, tokens), F32),
            pltpu.VMEM((units, tokens), F32),
            pltpu.VMEM((units, tokens), BF16),
            pltpu.VMEM((units, tokens), BF16),
            pltpu.SemaphoreType.DMA((8,)),
            pltpu.SemaphoreType.DMA((8,)),
            pltpu.SemaphoreType.DMA((3,)),
        ],
        name="step",
        compiler_params=pltpu.CompilerParams(vmem_limit_bytes=28 << 20),
        cost_estimate=pl.CostEstimate(
            flops=12 * size, bytes_accessed=16 << 20, transcendentals=2 * units * tokens
        ),
    )(*pieces, *weights)


def update_kernel(rate, squares, stack, grads, both, down):
    scale = rate[0] / jnp.sqrt(squares[0:1, 0:1] + 1e-06)

    def rows(block, _):
        at = pl.ds(pl.multiple_of(block * 32, 32), 32)
        for number in range(3):
            own, grad = stack[number, at].astype(F32), grads[number, at].astype(F32)
            to = both.at[number] if number < 2 else down
            to[at] = (own - scale * grad).astype(BF16)
        return 0

    lax.fori_loop(0, stack.shape[1] // 32, rows, 0)


def updated(rates, squares, stack, grads):
    return pl.pallas_call(
        update_kernel,
        out_shape=[pltpu.VMEM((2, *stack.shape[1:]), BF16), pltpu.VMEM(stack.shape[1:], BF16)],
        in_specs=[SMEM, VMEM, VMEM, VMEM],
        out_specs=[VMEM, VMEM],
        name="update",
        compiler_params=pltpu.CompilerParams(vmem_limit_bytes=18 << 20),
        cost_estimate=pl.CostEstimate(
            flops=2 * stack.size, bytes_accessed=6 * stack.size, transcendentals=0
        ),
    )(rates, squares, stack, grads)


def outputs_kernel(hidden1, hidden2, down1, stack2, kept, sent, passed, hidden, down, sems):
    me = lax.axis_index("tensor")
    pairs = [(hidden1, hidden.at[0]), (hidden2, hidden.at[1])]
    pairs += [(down1, down.at[0]), (stack2.at[2], down.at[1])]
    loads = [
        pltpu.make_async_copy(source, to, sems.at[number])
        for number, (source, to) in enumerate(pairs)
    ]
    for load in loads:
        load.start()
    for load in loads:
        load.wait()
    tokens = hidden.shape[2]
    width = kept.shape[2]
    y, xh = me // XH, me % XH

    def part(index, _):
        number, dxh = index // 2, index % 2
        rows = pl.ds(pl.multiple_of(number * tokens, tokens), tokens)
        outs = [
            (kept.at[dxh], y),
            (sent.at[0, dxh], y ^ 1),
            (sent.at[1, dxh], 3 - (y ^ 1)),
            (passed.at[dxh], 3 - y),
        ]
        for out, to in outs:
            place = (to * XH + (xh ^ dxh)) * width
            at = pl.ds(pl.multiple_of(place, width), width)
            out[rows] = contract(hidden[number], down[number, :, at], 0, 0).astype(BF16)
        return 0

    lax.fori_loop(0, 4, part, 0)


def outputs(hidden1, hidden2, down1, stack2):
    units, tokens = hidden1.shape
    features = down1.shape[1]
    block = (2, 2 * tokens, features // (Y * XH))
    return pl.pallas_call(
        outputs_kernel,
        out_shape=[
            jax.ShapeDtypeStruct(block, BF16),
            jax.ShapeDtypeStruct((2, *block), BF16),
            jax.ShapeDtypeStruct(block, BF16),
        ],
        in_specs=[ANY] * 4,
        out_specs=[VMEM] * 3,
        scratch_shapes=[
            pltpu.VMEM((2, units, tokens), BF16),
            pltpu.VMEM((2, units, features), BF16),
            pltpu.SemaphoreType.DMA((4,)),
        ],
        name="outputs",
        compiler_params=pltpu.CompilerParams(vmem_limit_bytes=20 << 20),
        cost_estimate=pl.CostEstimate(
            flops=4 * tokens * features * units, bytes_accessed=8 << 20, transcendentals=0
        ),
    )(hidden1, hidden2, down1, stack2)


def add_kernel(picks, *refs):
    *parts, out = refs
    shape = out.shape[:-2]

    def rows(block, _):
        at = pl.ds(pl.multiple_of(block * 32, 32), 32)
        for index in range(shape[0] if shape else 1):
            lead = (index,) if shape else ()
            total = sum(part[(*pick, *lead, at)].astype(F32) for part, pick in zip(parts, picks))
            out[(*lead, at)] = total.astype(out.dtype)
        return 0

    lax.fori_loop(0, out.shape[-2] // 32, rows, 0)


def add(*parts):
    arrays, picks = zip(*parts)
    shape = arrays[0].shape[len(picks[0]) :]
    return pl.pallas_call(
        partial(add_kernel, picks),
        out_shape=jax.ShapeDtypeStruct(shape, BF16),
        in_specs=[VMEM] * len(arrays),
        out_specs=VMEM,
        name="add",
        compiler_params=pltpu.CompilerParams(vmem_limit_bytes=20 << 20),
        cost_estimate=pl.CostEstimate(flops=1 << 20, bytes_accessed=4 << 20, transcendentals=0),
    )(*arrays)


def scatter_sum(kept, sent, passed):
    came = flip_y(sent, True)
    last = flip_y(add((passed, ()), (came, (1,))), False)
    across = flip_x(add((kept, (1,)), (came, (0, 1)), (last, (1,))))
    return add((kept, (0,)), (came, (0, 0)), (last, (0,)), (across, ()))


def scatter_sum_direct(kept, sent, passed, first):
    came = [flip_y(sent[0], True), flip_y(passed, False), shift_y(sent[1], 2)]
    came = lax.optimization_barrier((*came, *first))[:3]
    across = flip_x(add((kept, (1,)), *((part, (1,)) for part in came)))
    return add((kept, (0,)), *((part, (0,)) for part in came), (across, ()))


def group_sum(value, beside=None):
    value = value + flip_x(value)
    if beside is not None:
        value = after(value, *beside)
    value = value + flip_y(value, True)
    return value + flip_y(value, False), value


def swap(value, number):
    pairs = [(source, source ^ 2**number) for source in range(lax.axis_size("replica"))]
    return lax.ppermute(value, "replica", pairs)


def mean_kernel(fresh, other, *refs):
    *outs, theirs, in_sems, out_sems = refs
    count, rows = len(outs), outs[0].shape[0]
    half = rows // 2
    blocks = [(part, pl.ds(first, half)) for part in range(count) for first in (0, half)]

    def copy(number, out):
        part, at = blocks[number]
        if out:
            return pltpu.make_async_copy(
                theirs.at[part, at], outs[part].at[at], out_sems.at[number]
            )
        source = other.at[part, at] if count > 1 else other.at[at]
        return pltpu.make_async_copy(source, theirs.at[part, at], in_sems.at[number])

    for number in range(len(blocks)):
        copy(number, False).start()
    for number, (part, at) in enumerate(blocks):
        copy(number, False).wait()

        def some(index, _):
            at = pl.ds(pl.multiple_of((number % 2) * half + index * 16, 16), 16)
            own = fresh[part, at] if count > 1 else fresh[at]
            total = own.astype(F32) + theirs[part, at].astype(F32)
            theirs[part, at] = (total * 0.5).astype(BF16)
            return 0

        lax.fori_loop(0, half // 16, some, 0)
        copy(number, True).start()
    for number in range(len(blocks)):
        copy(number, True).wait()


def mean(fresh, other):
    count = fresh.shape[0] if fresh.ndim == 3 else 1
    shape = fresh.shape[-2:]
    return pl.pallas_call(
        mean_kernel,
        out_shape=[pltpu.HBM(shape, BF16)] * count,
        in_specs=[VMEM, ANY],
        out_specs=[ANY] * count,
        scratch_shapes=[
            pltpu.VMEM((count, *shape), BF16),
            pltpu.SemaphoreType.DMA((2 * count,)),
            pltpu.SemaphoreType.DMA((2 * count,)),
        ],
        name="mean",
        compiler_params=pltpu.CompilerParams(vmem_limit_bytes=10 << 20),
        cost_estimate=pl.CostEstimate(
            flops=2 * fresh.size, bytes_accessed=6 * fresh.size, transcendentals=0
        ),
    )(fresh, other)


def mix(number, both, down):
    others = swap(both, number), swap(down, number)
    first = mean(both, others[0])
    return first + mean(down, after(others[1], first[0]))


def mix_last(number, both, down, *blocks):
    new = mix(number, both, down)
    if number == 0:
        return new, scatter_sum_direct(*blocks, new)
    return new, scatter_sum(*blocks)


def by_bit(bit, handler, *values):
    return lax.switch(bit, [partial(handler, number) for number in range(4)], *values)


def after(value, *others):
    return lax.optimization_barrier((value, *others))[0]


def local(inputs, out_grads, gate_weight, up_weight, down_weight, rates, partner_bits):
    weights = [gate_weight[0].T, up_weight[0].T, down_weight[0]]
    weights[1] = pltpu.with_memory_space_constraint(weights[1], pltpu.HBM)
    own1 = jnp.concatenate([inputs[0], out_grads[0]])
    pieces1 = gather(own1)
    later = lax.optimization_barrier((inputs, out_grads, *pieces1[4:7]))
    own2 = jnp.concatenate([later[0][1], later[1][1]])
    near2 = gather_near(own2)

    stack, grads, hidden1, squares = step_pass(pieces1, weights, False)
    squares, partial_sum = group_sum(squares)
    near2 = list(lax.optimization_barrier((*near2, partial_sum))[:4])
    pieces2 = gather_across(own2, near2)
    pieces2 = [pltpu.with_memory_space_constraint(piece, pltpu.HBM) for piece in pieces2]
    fresh = updated(rates, squares, stack, grads)
    middle = by_bit(partner_bits[0], mix, *fresh)

    stack, grads, hidden2, squares = step_pass(pieces2, middle, True)
    blocks = outputs(hidden1, hidden2, weights[2], stack)
    squares, _ = group_sum(squares, blocks)
    fresh = updated(rates, squares, stack, grads)
    new, results = by_bit(partner_bits[1], mix_last, *fresh, *blocks)
    return (new[0].T[None], new[1].T[None], new[2][None], results.reshape(inputs.shape))


def solution(mesh):
    return jax.shard_map(
        local,
        mesh=mesh,
        in_specs=(
            P(None, "replica", "tensor"),
            P(None, "replica", "tensor"),
            P("replica", None, "tensor"),
            P("replica", None, "tensor"),
            P("replica", "tensor", None),
            P("replica"),
            P(),
        ),
        out_specs=(
            P("replica", None, "tensor"),
            P("replica", None, "tensor"),
            P("replica", "tensor", None),
            P(None, "replica", "tensor"),
        ),
        check_vma=False,
    )
```

```python
from functools import partial

import jax
import jax.numpy as jnp
from jax import lax
from jax.experimental import pallas as pl
from jax.experimental.pallas import tpu as pltpu
from jax.sharding import PartitionSpec as P


Y, XH = 4, 2
BF16, F32 = jnp.bfloat16, jnp.float32
ANY = pl.BlockSpec(memory_space=pl.ANY)
VMEM = pl.BlockSpec(memory_space=pltpu.VMEM)
SMEM = pl.BlockSpec(memory_space=pltpu.SMEM)


def tensor_permute(value, move):
    pairs = []
    for y in range(Y):
        for xh in range(XH):
            to_y, to_xh = move(y, xh)
            pairs.append((y * XH + xh, to_y % Y * XH + to_xh % XH))
    return lax.ppermute(value, "tensor", pairs)


def flip_x(value):
    return tensor_permute(value, lambda y, xh: (y, xh + 1))


def shift_y(value, by):
    return tensor_permute(value, lambda y, xh: (y + by, xh))


def flip_y(value, low):
    return tensor_permute(value, lambda y, xh: (y ^ 1 if low else 3 - y, xh))


def place(me, dy, dxh):
    return ((me + dy * XH) & (Y * XH - XH)) | ((me + dxh) & (XH - 1))


def gather(own):
    below = shift_y(own, 1)
    above = shift_y(own, -1)
    other = flip_x(own)
    far = shift_y(own, 2)
    other, below, above = lax.optimization_barrier((other, below, above))
    return [own, other, below, above, shift_y(other, 1), shift_y(other, -1), far, flip_x(far)]


def gather_near(own):
    return [flip_x(own), shift_y(own, 1), shift_y(own, -1), shift_y(own, 2)]


def gather_across(own, near):
    other, below, above, far = near
    theirs = jnp.stack([below, above, far])
    theirs = flip_x(theirs)
    return [own, other, below, above, far, theirs]


PIECES = [(0, 0), (0, 1), (-1, 0), (1, 0), (-1, 1), (1, 1), (2, 0), (2, 1)]


def fetch(me, pieces, first, out, sems):
    rows = out.shape[0]
    width = out.shape[1] // (Y * XH)
    copies = []
    for number, (piece, (dy, dxh)) in enumerate(zip(pieces, PIECES)):
        at = pl.multiple_of(place(me, dy, dxh) * width, width)
        copies.append(
            pltpu.make_async_copy(
                piece.at[pl.ds(first, rows)], out.at[:, pl.ds(at, width)], sems.at[number]
            )
        )
    for copy in copies:
        copy.start()
    return copies


def contract(a, b, dim_a, dim_b):
    return lax.dot_general(
        a, b, (((dim_a,), (dim_b,)), ((), ())), preferred_element_type=F32
    )


def step_kernel(second, *refs):
    if second:
        own, flipped, below, above, far, across, *refs = refs
        pieces = [own, flipped, below, above, across.at[0], across.at[1], far, across.at[2]]
    else:
        pieces, refs = refs[:8], refs[8:]
    sources, refs = refs[:3], refs[3:]
    weights, grads, hidden, squares_out, *refs = refs
    x, dy, gates, ups, d_gate, d_up, x_sems, dy_sems, w_sems = refs
    tokens, features = x.shape
    me = lax.axis_index("tensor")

    def load(number):
        copy = pltpu.make_async_copy(sources[number], weights.at[number], w_sems.at[number])
        copy.start()
        return copy

    loads = [load(0)]
    x_copies = fetch(me, pieces, 0, x, x_sems)
    loads += [load(1), load(2)]
    dy_copies = fetch(me, pieces, tokens, dy, dy_sems)

    chunk = 256
    wide = 512

    def over_tokens(body):
        def step(block, _):
            body(pl.ds(pl.multiple_of(block * chunk, chunk), chunk))
            return 0

        lax.fori_loop(0, tokens // chunk, step, 0)

    def gate_pass(at):
        gates[:, at] = contract(weights[0], x[at], 1, 1)

    def up_pass(at):
        up = contract(weights[1], x[at], 1, 1)
        gate = gates[:, at]
        ups[:, at] = up
        hidden[:, at] = (gate * jax.nn.sigmoid(gate) * up).astype(BF16)

    def back_pass(at):
        back = contract(weights[2], dy[at], 1, 1)
        gate = gates[:, at]
        sigma = jax.nn.sigmoid(gate)
        d_gate[:, at] = (
            back * ups[:, at] * sigma * (1.0 + gate * (1.0 - sigma))
        ).astype(BF16)
        d_up[:, at] = (back * (gate * sigma)).astype(BF16)

    loads[0].wait()
    for copy in x_copies:
        copy.wait()
    over_tokens(gate_pass)
    loads[1].wait()
    over_tokens(up_pass)
    loads[2].wait()
    for copy in dy_copies:
        copy.wait()
    over_tokens(back_pass)

    def columns(block, total):
        at = pl.ds(pl.multiple_of(block * wide, wide), wide)
        for number, (left, right) in enumerate([(d_gate, x), (d_up, x), (hidden, dy)]):
            grad = contract(left[...], right[:, at], 1, 0)
            grads[number, :, at] = grad.astype(BF16)
            total = total + jnp.sum(grad * grad, axis=0, keepdims=True)
        return total

    blocks = features // wide
    total = lax.fori_loop(0, blocks, columns, jnp.zeros((1, wide), F32))
    squares_out[...] = jnp.broadcast_to(jnp.sum(total, axis=1, keepdims=True), (8, 128))


def step_pass(pieces, weights, second):
    rows, width = pieces[0].shape
    tokens = rows // 2
    features = width * Y * XH
    units = weights[0].shape[-2]
    size = tokens * features * units
    stack = (3, units, features)
    return pl.pallas_call(
        partial(step_kernel, second),
        out_shape=[
            pltpu.VMEM(stack, BF16),
            pltpu.VMEM(stack, BF16),
            jax.ShapeDtypeStruct((units, tokens), BF16),
            jax.ShapeDtypeStruct((8, 128), F32),
        ],
        in_specs=[ANY] * (len(pieces) + len(weights)),
        out_specs=[VMEM] * 4,
        scratch_shapes=[
            pltpu.VMEM((tokens, features), BF16),
            pltpu.VMEM((tokens, features), BF16),
            pltpu.VMEM((units, tokens), F32),
            pltpu.VMEM((units, tokens), F32),
            pltpu.VMEM((units, tokens), BF16),
            pltpu.VMEM((units, tokens), BF16),
            pltpu.SemaphoreType.DMA((8,)),
            pltpu.SemaphoreType.DMA((8,)),
            pltpu.SemaphoreType.DMA((3,)),
        ],
        name="step",
        compiler_params=pltpu.CompilerParams(vmem_limit_bytes=28 << 20),
        cost_estimate=pl.CostEstimate(
            flops=12 * size, bytes_accessed=16 << 20, transcendentals=2 * units * tokens
        ),
    )(*pieces, *weights)


def update_kernel(rate, squares, stack, grads, both, down):
    scale = rate[0] / jnp.sqrt(squares[0:1, 0:1] + 1e-06)

    def rows(block, _):
        at = pl.ds(pl.multiple_of(block * 32, 32), 32)
        for number in range(3):
            own, grad = stack[number, at].astype(F32), grads[number, at].astype(F32)
            to = both.at[number] if number < 2 else down
            to[at] = (own - scale * grad).astype(BF16)
        return 0

    lax.fori_loop(0, stack.shape[1] // 32, rows, 0)


def updated(rates, squares, stack, grads):
    return pl.pallas_call(
        update_kernel,
        out_shape=[pltpu.VMEM((2, *stack.shape[1:]), BF16), pltpu.VMEM(stack.shape[1:], BF16)],
        in_specs=[SMEM, VMEM, VMEM, VMEM],
        out_specs=[VMEM, VMEM],
        name="update",
        compiler_params=pltpu.CompilerParams(vmem_limit_bytes=18 << 20),
        cost_estimate=pl.CostEstimate(
            flops=2 * stack.size, bytes_accessed=6 * stack.size, transcendentals=0
        ),
    )(rates, squares, stack, grads)


def outputs_kernel(hidden1, hidden2, down1, stack2, kept, sent, passed, hidden, down, sems):
    me = lax.axis_index("tensor")
    pairs = [(hidden1, hidden.at[0]), (hidden2, hidden.at[1])]
    pairs += [(down1, down.at[0]), (stack2.at[2], down.at[1])]
    loads = [
        pltpu.make_async_copy(source, to, sems.at[number])
        for number, (source, to) in enumerate(pairs)
    ]
    for load in loads:
        load.start()
    for load in loads:
        load.wait()
    tokens = hidden.shape[2]
    width = kept.shape[2]
    y, xh = me // XH, me % XH

    def part(index, _):
        number, dxh = index // 2, index % 2
        rows = pl.ds(pl.multiple_of(number * tokens, tokens), tokens)
        outs = [
            (kept.at[dxh], y),
            (sent.at[0, dxh], y ^ 1),
            (sent.at[1, dxh], 3 - (y ^ 1)),
            (passed.at[dxh], 3 - y),
        ]
        for out, to in outs:
            place = (to * XH + (xh ^ dxh)) * width
            at = pl.ds(pl.multiple_of(place, width), width)
            out[rows] = contract(hidden[number], down[number, :, at], 0, 0).astype(BF16)
        return 0

    lax.fori_loop(0, 4, part, 0)


def outputs(hidden1, hidden2, down1, stack2):
    units, tokens = hidden1.shape
    features = down1.shape[1]
    block = (2, 2 * tokens, features // (Y * XH))
    return pl.pallas_call(
        outputs_kernel,
        out_shape=[
            jax.ShapeDtypeStruct(block, BF16),
            jax.ShapeDtypeStruct((2, *block), BF16),
            jax.ShapeDtypeStruct(block, BF16),
        ],
        in_specs=[ANY] * 4,
        out_specs=[VMEM] * 3,
        scratch_shapes=[
            pltpu.VMEM((2, units, tokens), BF16),
            pltpu.VMEM((2, units, features), BF16),
            pltpu.SemaphoreType.DMA((4,)),
        ],
        name="outputs",
        compiler_params=pltpu.CompilerParams(vmem_limit_bytes=20 << 20),
        cost_estimate=pl.CostEstimate(
            flops=4 * tokens * features * units, bytes_accessed=8 << 20, transcendentals=0
        ),
    )(hidden1, hidden2, down1, stack2)


def add_kernel(groups, *refs):
    *arrays, out = refs
    lead = out.shape[:-2]
    rows = out.shape[-2] // len(groups)
    for number, group in enumerate(groups):

        def some(block, _):
            for index in [(k,) for k in range(lead[0])] if lead else [()]:
                total = 0.0
                for which, pick, first in group:
                    at = pl.ds(pl.multiple_of(first + block * 32, 32), 32)
                    total = total + arrays[which][(*pick, *index, at)].astype(F32)
                at = pl.ds(pl.multiple_of(number * rows + block * 32, 32), 32)
                out[(*index, at)] = total.astype(out.dtype)
            return 0

        lax.fori_loop(0, rows // 32, some, 0)


def add_groups(arrays, groups, shape):
    return pl.pallas_call(
        partial(add_kernel, groups),
        out_shape=jax.ShapeDtypeStruct(shape, BF16),
        in_specs=[VMEM] * len(arrays),
        out_specs=VMEM,
        name="add",
        compiler_params=pltpu.CompilerParams(vmem_limit_bytes=20 << 20),
        cost_estimate=pl.CostEstimate(flops=1 << 20, bytes_accessed=4 << 20, transcendentals=0),
    )(*arrays)


def add(*parts):
    arrays = [array for array, _ in parts]
    group = [(number, pick, 0) for number, (_, pick) in enumerate(parts)]
    return add_groups(arrays, [group], arrays[0].shape[len(parts[0][1]) :])


def scatter_sum(kept, sent, passed):
    came = flip_y(sent, True)
    last = flip_y(add((passed, ()), (came, (1,))), False)
    across = flip_x(add((kept, (1,)), (came, (0, 1)), (last, (1,))))
    return add((kept, (0,)), (came, (0, 0)), (last, (0,)), (across, ()))


def split_kernel(kept, sent, passed, *outs):
    *firsts, others = outs
    rows = others.shape[1]
    blocks = [sent.at[0], passed, sent.at[1]]

    def some(block, _):
        at = pl.ds(pl.multiple_of(block * 32, 32), 32)
        later = pl.ds(pl.multiple_of(rows + block * 32, 32), 32)
        for out, source in zip(firsts, blocks):
            for dxh in range(2):
                out[dxh, at] = source[dxh, at]
        for number, source in enumerate([kept, *blocks]):
            others[number, at] = source[1, later]
        return 0

    lax.fori_loop(0, rows // 32, some, 0)


def scatter_sum_direct(kept, sent, passed, first):
    _, rows, width = kept.shape
    half = rows // 2
    *starts, others = pl.pallas_call(
        split_kernel,
        out_shape=[jax.ShapeDtypeStruct((2, half, width), BF16)] * 3
        + [jax.ShapeDtypeStruct((4, half, width), BF16)],
        in_specs=[VMEM] * 3,
        out_specs=[VMEM] * 4,
        name="split",
        compiler_params=pltpu.CompilerParams(vmem_limit_bytes=24 << 20),
        cost_estimate=pl.CostEstimate(flops=1 << 20, bytes_accessed=8 << 20, transcendentals=0),
    )(kept, sent, passed)

    def spread(parts):
        return [flip_y(parts[0], True), flip_y(parts[1], False), shift_y(parts[2], 2)]

    came = spread(starts)
    theirs = flip_x(others)
    *came, theirs = lax.optimization_barrier((*came, theirs, *first))[:4]
    block = (half, width)
    ways = [(sent, (0, 0)), (passed, (0,)), (sent, (1, 0))]
    sums = [
        add_groups([array, theirs], [[(0, pick, half), (1, (number,), 0)]], block)
        for number, (array, pick) in enumerate(ways, 1)
    ]
    late = spread(sums)
    ends = [(number, (1,), 0) for number in range(4)]
    across = flip_x(add_groups([kept, *came], [ends], block))
    top = [(0, (0,), 0), (1, (0,), 0), (2, (0,), 0), (3, (0,), 0), (4, (), 0)]
    low = [(0, (0,), half), (5, (0,), 0), (6, (), 0), (7, (), 0), (8, (), 0)]
    return add_groups([kept, *came, across, theirs, *late], [top, low], (rows, width))


def group_sum(value, beside=None):
    value = value + flip_x(value)
    if beside is not None:
        value = after(value, *beside)
    value = value + flip_y(value, True)
    return value + flip_y(value, False), value


def swap(value, number):
    pairs = [(source, source ^ 2**number) for source in range(lax.axis_size("replica"))]
    return lax.ppermute(value, "replica", pairs)


def mean_kernel(fresh, other, *refs):
    *outs, theirs, in_sems, out_sems = refs
    count, (rows, columns) = len(outs), outs[0].shape
    half, wide = rows // 2, columns // 2

    def copies(part, side):
        at = pl.ds(pl.multiple_of(side * half, 16), half)
        number = 2 * part + side
        source = other.at[part, at] if count > 1 else other.at[at]
        slot = theirs.at[part, at]
        return (
            pltpu.make_async_copy(source, slot, in_sems.at[number]),
            pltpu.make_async_copy(slot, outs[part].at[at], out_sems.at[number]),
        )

    for part in range(count):
        for side in range(2):
            copies(part, side)[0].start()
    for part in range(count):

        def piece(side, _):
            load, store = copies(part, side)
            load.wait()

            def some(index, _):
                at = pl.ds(pl.multiple_of(side * half + index // 2 * 16, 16), 16)
                to = pl.ds(pl.multiple_of(index % 2 * wide, wide), wide)
                own = fresh[part, at, to] if count > 1 else fresh[at, to]
                total = own.astype(F32) + theirs[part, at, to].astype(F32)
                theirs[part, at, to] = (total * 0.5).astype(BF16)
                return 0

            lax.fori_loop(0, half // 16 * 2, some, 0)
            store.start()
            return 0

        lax.fori_loop(0, 2, piece, 0)
    for part in range(count):
        for side in range(2):
            copies(part, side)[1].wait()


def mean(fresh, other):
    count = fresh.shape[0] if fresh.ndim == 3 else 1
    shape = fresh.shape[-2:]
    return pl.pallas_call(
        mean_kernel,
        out_shape=[pltpu.HBM(shape, BF16)] * count,
        in_specs=[VMEM, ANY],
        out_specs=[ANY] * count,
        scratch_shapes=[
            pltpu.VMEM((count, *shape), BF16),
            pltpu.SemaphoreType.DMA((2 * count,)),
            pltpu.SemaphoreType.DMA((2 * count,)),
        ],
        name="mean",
        compiler_params=pltpu.CompilerParams(vmem_limit_bytes=10 << 20),
        cost_estimate=pl.CostEstimate(
            flops=2 * fresh.size, bytes_accessed=6 * fresh.size, transcendentals=0
        ),
    )(fresh, other)


def mix(number, both, down):
    others = swap(both, number), swap(down, number)
    first = mean(both, others[0])
    return first + mean(down, after(others[1], first[0]))


def mix_last(number, both, down, *blocks):
    new = mix(number, both, down)
    if number == 0:
        return new, scatter_sum_direct(*blocks, new)
    return new, scatter_sum(*blocks)


def by_bit(bit, handler, *values):
    return lax.switch(bit, [partial(handler, number) for number in range(4)], *values)


def after(value, *others):
    return lax.optimization_barrier((value, *others))[0]


def local(inputs, out_grads, gate_weight, up_weight, down_weight, rates, partner_bits):
    weights = [gate_weight[0].T, up_weight[0].T, down_weight[0]]
    weights[1] = pltpu.with_memory_space_constraint(weights[1], pltpu.HBM)
    own1 = jnp.concatenate([inputs[0], out_grads[0]])
    pieces1 = gather(own1)
    later = lax.optimization_barrier((inputs, out_grads, *pieces1[4:7]))
    own2 = jnp.concatenate([later[0][1], later[1][1]])
    near2 = gather_near(own2)

    stack, grads, hidden1, squares = step_pass(pieces1, weights, False)
    squares, partial_sum = group_sum(squares)
    near2 = list(lax.optimization_barrier((*near2, partial_sum))[:4])
    pieces2 = gather_across(own2, near2)
    pieces2 = [pltpu.with_memory_space_constraint(piece, pltpu.HBM) for piece in pieces2]
    fresh = updated(rates, squares, stack, grads)
    middle = by_bit(partner_bits[0], mix, *fresh)

    stack, grads, hidden2, squares = step_pass(pieces2, middle, True)
    blocks = outputs(hidden1, hidden2, weights[2], stack)
    squares, _ = group_sum(squares, blocks)
    fresh = updated(rates, squares, stack, grads)
    new, results = by_bit(partner_bits[1], mix_last, *fresh, *blocks)
    return (new[0].T[None], new[1].T[None], new[2][None], results.reshape(inputs.shape))


def solution(mesh):
    return jax.shard_map(
        local,
        mesh=mesh,
        in_specs=(
            P(None, "replica", "tensor"),
            P(None, "replica", "tensor"),
            P("replica", None, "tensor"),
            P("replica", None, "tensor"),
            P("replica", "tensor", None),
            P("replica"),
            P(),
        ),
        out_specs=(
            P("replica", None, "tensor"),
            P("replica", None, "tensor"),
            P("replica", "tensor", None),
            P(None, "replica", "tensor"),
        ),
        check_vma=False,
    )
```

```python
from functools import partial

import jax
import jax.numpy as jnp
from jax import lax
from jax.experimental import pallas as pl
from jax.experimental.pallas import tpu as pltpu
from jax.sharding import PartitionSpec as P


Y, XH = 4, 2
BF16, F32 = jnp.bfloat16, jnp.float32
ANY = pl.BlockSpec(memory_space=pl.ANY)
VMEM = pl.BlockSpec(memory_space=pltpu.VMEM)
SMEM = pl.BlockSpec(memory_space=pltpu.SMEM)


def tensor_permute(value, move):
    pairs = []
    for y in range(Y):
        for xh in range(XH):
            to_y, to_xh = move(y, xh)
            pairs.append((y * XH + xh, to_y % Y * XH + to_xh % XH))
    return lax.ppermute(value, "tensor", pairs)


def flip_x(value):
    return tensor_permute(value, lambda y, xh: (y, xh + 1))


def shift_y(value, by):
    return tensor_permute(value, lambda y, xh: (y + by, xh))


def flip_y(value, low):
    return tensor_permute(value, lambda y, xh: (y ^ 1 if low else 3 - y, xh))


def place(me, dy, dxh):
    return ((me + dy * XH) & (Y * XH - XH)) | ((me + dxh) & (XH - 1))


def gather(own):
    far = shift_y(own, 2)
    other = flip_x(own)
    other, far = lax.optimization_barrier((other, far))
    column = jnp.stack([own, other])
    return [own, other, shift_y(column, 1), shift_y(column, -1), far, flip_x(far)]


def gather_near(own):
    return [flip_x(own), shift_y(own, 1), shift_y(own, -1), shift_y(own, 2)]


def gather_across(own, near):
    other, below, above, far = near
    theirs = jnp.stack([below, above, far])
    theirs = flip_x(theirs)
    return [own, other, below, above, far, theirs]


PIECES = [(0, 0), (0, 1), (-1, 0), (1, 0), (-1, 1), (1, 1), (2, 0), (2, 1)]


def fetch(me, pieces, first, out, sems):
    rows = out.shape[0]
    width = out.shape[1] // (Y * XH)
    copies = []
    for number, (piece, (dy, dxh)) in enumerate(zip(pieces, PIECES)):
        at = pl.multiple_of(place(me, dy, dxh) * width, width)
        copies.append(
            pltpu.make_async_copy(
                piece.at[pl.ds(first, rows)], out.at[:, pl.ds(at, width)], sems.at[number]
            )
        )
    for copy in copies:
        copy.start()
    return copies


def contract(a, b, dim_a, dim_b):
    return lax.dot_general(
        a, b, (((dim_a,), (dim_b,)), ((), ())), preferred_element_type=F32
    )


def step_kernel(second, *refs):
    if second:
        own, flipped, below, above, far, across, *refs = refs
        pieces = [own, flipped, below, above, across.at[0], across.at[1], far, across.at[2]]
    else:
        own, flipped, below, above, far, across, *refs = refs
        pieces = [own, flipped, below.at[0], above.at[0], below.at[1], above.at[1], far, across]
    sources, refs = refs[:3], refs[3:]
    weights, grads, hidden, squares_out, *refs = refs
    x, dy, gates, ups, d_gate, d_up, x_sems, dy_sems, w_sems = refs
    tokens, features = x.shape
    me = lax.axis_index("tensor")

    def load(number):
        copy = pltpu.make_async_copy(sources[number], weights.at[number], w_sems.at[number])
        copy.start()
        return copy

    loads = [load(0)]
    x_copies = fetch(me, pieces, 0, x, x_sems)
    loads += [load(1), load(2)]
    dy_copies = fetch(me, pieces, tokens, dy, dy_sems)

    chunk = 256
    wide = 256

    def over_tokens(body):
        def step(block, _):
            body(pl.ds(pl.multiple_of(block * chunk, chunk), chunk))
            return 0

        lax.fori_loop(0, tokens // chunk, step, 0)

    def gate_pass(at):
        gates[:, at] = contract(weights[0], x[at], 1, 1)

    def up_pass(at):
        up = contract(weights[1], x[at], 1, 1)
        gate = gates[:, at]
        ups[:, at] = up
        hidden[:, at] = (gate * jax.nn.sigmoid(gate) * up).astype(BF16)

    def back_pass(at):
        back = contract(weights[2], dy[at], 1, 1)
        gate = gates[:, at]
        sigma = jax.nn.sigmoid(gate)
        d_gate[:, at] = (
            back * ups[:, at] * sigma * (1.0 + gate * (1.0 - sigma))
        ).astype(BF16)
        d_up[:, at] = (back * (gate * sigma)).astype(BF16)

    loads[0].wait()
    for copy in x_copies:
        copy.wait()
    over_tokens(gate_pass)
    loads[1].wait()
    over_tokens(up_pass)
    loads[2].wait()
    for copy in dy_copies:
        copy.wait()
    over_tokens(back_pass)

    def columns(block, total):
        at = pl.ds(pl.multiple_of(block * wide, wide), wide)
        for number, (left, right) in enumerate([(d_gate, x), (d_up, x), (hidden, dy)]):
            grad = contract(left[...], right[:, at], 1, 0)
            grads[number, :, at] = grad.astype(BF16)
            total = total + jnp.sum(grad * grad, axis=0, keepdims=True)
        return total

    blocks = features // wide
    total = lax.fori_loop(0, blocks, columns, jnp.zeros((1, wide), F32))
    squares_out[...] = jnp.broadcast_to(jnp.sum(total, axis=1, keepdims=True), (8, 128))


def step_pass(pieces, weights, second):
    rows, width = pieces[0].shape
    tokens = rows // 2
    features = width * Y * XH
    units = weights[0].shape[-2]
    size = tokens * features * units
    stack = (3, units, features)
    return pl.pallas_call(
        partial(step_kernel, second),
        out_shape=[
            pltpu.VMEM(stack, BF16),
            pltpu.VMEM(stack, BF16),
            jax.ShapeDtypeStruct((units, tokens), BF16),
            jax.ShapeDtypeStruct((8, 128), F32),
        ],
        in_specs=[ANY] * (len(pieces) + len(weights)),
        out_specs=[VMEM] * 4,
        scratch_shapes=[
            pltpu.VMEM((tokens, features), BF16),
            pltpu.VMEM((tokens, features), BF16),
            pltpu.VMEM((units, tokens), F32),
            pltpu.VMEM((units, tokens), F32),
            pltpu.VMEM((units, tokens), BF16),
            pltpu.VMEM((units, tokens), BF16),
            pltpu.SemaphoreType.DMA((8,)),
            pltpu.SemaphoreType.DMA((8,)),
            pltpu.SemaphoreType.DMA((3,)),
        ],
        name="step",
        compiler_params=pltpu.CompilerParams(vmem_limit_bytes=28 << 20),
        cost_estimate=pl.CostEstimate(
            flops=12 * size, bytes_accessed=16 << 20, transcendentals=2 * units * tokens
        ),
    )(*pieces, *weights)


def update_kernel(rate, squares, stack, grads, both, down):
    scale = rate[0] / jnp.sqrt(squares[0:1, 0:1] + 1e-06)

    def rows(block, _):
        at = pl.ds(pl.multiple_of(block * 32, 32), 32)
        for number in range(3):
            own, grad = stack[number, at].astype(F32), grads[number, at].astype(F32)
            to = both.at[number] if number < 2 else down
            to[at] = (own - scale * grad).astype(BF16)
        return 0

    lax.fori_loop(0, stack.shape[1] // 32, rows, 0)


def updated(rates, squares, stack, grads):
    return pl.pallas_call(
        update_kernel,
        out_shape=[pltpu.VMEM((2, *stack.shape[1:]), BF16), pltpu.VMEM(stack.shape[1:], BF16)],
        in_specs=[SMEM, VMEM, VMEM, VMEM],
        out_specs=[VMEM, VMEM],
        name="update",
        compiler_params=pltpu.CompilerParams(vmem_limit_bytes=18 << 20),
        cost_estimate=pl.CostEstimate(
            flops=2 * stack.size, bytes_accessed=6 * stack.size, transcendentals=0
        ),
    )(rates, squares, stack, grads)


def outputs_kernel(hidden1, hidden2, down1, stack2, kept, sent, passed, hidden, down, sems):
    me = lax.axis_index("tensor")
    pairs = [(hidden1, hidden.at[0]), (hidden2, hidden.at[1])]
    pairs += [(down1, down.at[0]), (stack2.at[2], down.at[1])]
    loads = [
        pltpu.make_async_copy(source, to, sems.at[number])
        for number, (source, to) in enumerate(pairs)
    ]
    for load in loads:
        load.start()
    for load in loads:
        load.wait()
    tokens = hidden.shape[2]
    width = kept.shape[2]
    y, xh = me // XH, me % XH

    def part(index, _):
        number, dxh = index // 2, index % 2
        rows = pl.ds(pl.multiple_of(number * tokens, tokens), tokens)
        outs = [
            (kept.at[dxh], y),
            (sent.at[0, dxh], y ^ 1),
            (sent.at[1, dxh], 3 - (y ^ 1)),
            (passed.at[dxh], 3 - y),
        ]
        for out, to in outs:
            place = (to * XH + (xh ^ dxh)) * width
            at = pl.ds(pl.multiple_of(place, width), width)
            out[rows] = contract(hidden[number], down[number, :, at], 0, 0).astype(BF16)
        return 0

    lax.fori_loop(0, 4, part, 0)


def outputs(hidden1, hidden2, down1, stack2):
    units, tokens = hidden1.shape
    features = down1.shape[1]
    block = (2, 2 * tokens, features // (Y * XH))
    return pl.pallas_call(
        outputs_kernel,
        out_shape=[
            jax.ShapeDtypeStruct(block, BF16),
            jax.ShapeDtypeStruct((2, *block), BF16),
            jax.ShapeDtypeStruct(block, BF16),
        ],
        in_specs=[ANY] * 4,
        out_specs=[VMEM] * 3,
        scratch_shapes=[
            pltpu.VMEM((2, units, tokens), BF16),
            pltpu.VMEM((2, units, features), BF16),
            pltpu.SemaphoreType.DMA((4,)),
        ],
        name="outputs",
        compiler_params=pltpu.CompilerParams(vmem_limit_bytes=20 << 20),
        cost_estimate=pl.CostEstimate(
            flops=4 * tokens * features * units, bytes_accessed=8 << 20, transcendentals=0
        ),
    )(hidden1, hidden2, down1, stack2)


def add_kernel(groups, *refs):
    *arrays, out = refs
    lead = out.shape[:-2]
    rows = out.shape[-2] // len(groups)
    for number, group in enumerate(groups):

        def some(block, _):
            for index in [(k,) for k in range(lead[0])] if lead else [()]:
                total = 0.0
                for which, pick, first in group:
                    at = pl.ds(pl.multiple_of(first + block * 32, 32), 32)
                    total = total + arrays[which][(*pick, *index, at)].astype(F32)
                at = pl.ds(pl.multiple_of(number * rows + block * 32, 32), 32)
                out[(*index, at)] = total.astype(out.dtype)
            return 0

        lax.fori_loop(0, rows // 32, some, 0)


def add_groups(arrays, groups, shape):
    return pl.pallas_call(
        partial(add_kernel, groups),
        out_shape=jax.ShapeDtypeStruct(shape, BF16),
        in_specs=[VMEM] * len(arrays),
        out_specs=VMEM,
        name="add",
        compiler_params=pltpu.CompilerParams(vmem_limit_bytes=20 << 20),
        cost_estimate=pl.CostEstimate(flops=1 << 20, bytes_accessed=4 << 20, transcendentals=0),
    )(*arrays)


def add(*parts):
    arrays = [array for array, _ in parts]
    group = [(number, pick, 0) for number, (_, pick) in enumerate(parts)]
    return add_groups(arrays, [group], arrays[0].shape[len(parts[0][1]) :])


def scatter_sum(kept, sent, passed):
    came = flip_y(sent, True)
    last = flip_y(add((passed, ()), (came, (1,))), False)
    across = flip_x(add((kept, (1,)), (came, (0, 1)), (last, (1,))))
    return add((kept, (0,)), (came, (0, 0)), (last, (0,)), (across, ()))


def split_kernel(kept, sent, passed, *outs):
    *firsts, others = outs
    rows = others.shape[1]
    blocks = [sent.at[0], passed, sent.at[1]]

    def some(block, _):
        at = pl.ds(pl.multiple_of(block * 32, 32), 32)
        later = pl.ds(pl.multiple_of(rows + block * 32, 32), 32)
        for out, source in zip(firsts, blocks):
            for dxh in range(2):
                out[dxh, at] = source[dxh, at]
        for number, source in enumerate([kept, *blocks]):
            others[number, at] = source[1, later]
        return 0

    lax.fori_loop(0, rows // 32, some, 0)


def scatter_sum_direct(kept, sent, passed, first):
    _, rows, width = kept.shape
    half = rows // 2
    *starts, others = pl.pallas_call(
        split_kernel,
        out_shape=[jax.ShapeDtypeStruct((2, half, width), BF16)] * 3
        + [jax.ShapeDtypeStruct((4, half, width), BF16)],
        in_specs=[VMEM] * 3,
        out_specs=[VMEM] * 4,
        name="split",
        compiler_params=pltpu.CompilerParams(vmem_limit_bytes=24 << 20),
        cost_estimate=pl.CostEstimate(flops=1 << 20, bytes_accessed=8 << 20, transcendentals=0),
    )(kept, sent, passed)

    def spread(parts):
        return [flip_y(parts[0], True), flip_y(parts[1], False), shift_y(parts[2], 2)]

    came = spread(starts)
    theirs = flip_x(others)
    *came, theirs = lax.optimization_barrier((*came, theirs, *first))[:4]
    block = (half, width)
    ways = [(sent, (0, 0)), (passed, (0,)), (sent, (1, 0))]
    sums = [
        add_groups([array, theirs], [[(0, pick, half), (1, (number,), 0)]], block)
        for number, (array, pick) in enumerate(ways, 1)
    ]
    late = spread(sums)
    ends = [(number, (1,), 0) for number in range(4)]
    across = flip_x(add_groups([kept, *came], [ends], block))
    top = [(0, (0,), 0), (1, (0,), 0), (2, (0,), 0), (3, (0,), 0), (4, (), 0)]
    low = [(0, (0,), half), (5, (0,), 0), (6, (), 0), (7, (), 0), (8, (), 0)]
    return add_groups([kept, *came, across, theirs, *late], [top, low], (rows, width))


def group_sum(value, beside=None):
    value = value + flip_x(value)
    if beside is not None:
        value = after(value, *beside)
    value = value + flip_y(value, True)
    return value + flip_y(value, False), value


def swap(value, number):
    pairs = [(source, source ^ 2**number) for source in range(lax.axis_size("replica"))]
    return lax.ppermute(value, "replica", pairs)


def mean_kernel(fresh, other, *refs):
    *outs, theirs, in_sems, out_sems = refs
    count, (rows, columns) = len(outs), outs[0].shape
    half, wide = rows // 2, columns // 2

    def copies(part, side):
        at = pl.ds(pl.multiple_of(side * half, 16), half)
        number = 2 * part + side
        source = other.at[part, at] if count > 1 else other.at[at]
        slot = theirs.at[part, at]
        return (
            pltpu.make_async_copy(source, slot, in_sems.at[number]),
            pltpu.make_async_copy(slot, outs[part].at[at], out_sems.at[number]),
        )

    for part in range(count):
        for side in range(2):
            copies(part, side)[0].start()
    for part in range(count):

        def piece(side, _):
            load, store = copies(part, side)
            load.wait()

            def some(index, _):
                at = pl.ds(pl.multiple_of(side * half + index // 2 * 16, 16), 16)
                to = pl.ds(pl.multiple_of(index % 2 * wide, wide), wide)
                own = fresh[part, at, to] if count > 1 else fresh[at, to]
                total = own.astype(F32) + theirs[part, at, to].astype(F32)
                theirs[part, at, to] = (total * 0.5).astype(BF16)
                return 0

            lax.fori_loop(0, half // 16 * 2, some, 0)
            store.start()
            return 0

        lax.fori_loop(0, 2, piece, 0)
    for part in range(count):
        for side in range(2):
            copies(part, side)[1].wait()


def mean(fresh, other):
    count = fresh.shape[0] if fresh.ndim == 3 else 1
    shape = fresh.shape[-2:]
    return pl.pallas_call(
        mean_kernel,
        out_shape=[pltpu.HBM(shape, BF16)] * count,
        in_specs=[VMEM, ANY],
        out_specs=[ANY] * count,
        scratch_shapes=[
            pltpu.VMEM((count, *shape), BF16),
            pltpu.SemaphoreType.DMA((2 * count,)),
            pltpu.SemaphoreType.DMA((2 * count,)),
        ],
        name="mean",
        compiler_params=pltpu.CompilerParams(vmem_limit_bytes=10 << 20),
        cost_estimate=pl.CostEstimate(
            flops=2 * fresh.size, bytes_accessed=6 * fresh.size, transcendentals=0
        ),
    )(fresh, other)


def mix(number, both, down):
    others = swap(both, number), swap(down, number)
    first = mean(both, others[0])
    return first + mean(down, after(others[1], first[0]))


def mix_last(number, both, down, *blocks):
    new = mix(number, both, down)
    if number == 0:
        return new, scatter_sum_direct(*blocks, new)
    return new, scatter_sum(*blocks)


def by_bit(bit, handler, *values):
    return lax.switch(bit, [partial(handler, number) for number in range(4)], *values)


def after(value, *others):
    return lax.optimization_barrier((value, *others))[0]


def local(inputs, out_grads, gate_weight, up_weight, down_weight, rates, partner_bits):
    weights = [gate_weight[0].T, up_weight[0].T, down_weight[0]]
    weights[1] = pltpu.with_memory_space_constraint(weights[1], pltpu.HBM)
    own1 = jnp.concatenate([inputs[0], out_grads[0]])
    pieces1 = gather(own1)
    later = lax.optimization_barrier((inputs, out_grads, *pieces1[2:5]))
    own2 = jnp.concatenate([later[0][1], later[1][1]])
    near2 = gather_near(own2)

    stack, grads, hidden1, squares = step_pass(pieces1, weights, False)
    squares, partial_sum = group_sum(squares)
    near2 = list(lax.optimization_barrier((*near2, partial_sum))[:4])
    pieces2 = gather_across(own2, near2)
    pieces2 = [pltpu.with_memory_space_constraint(piece, pltpu.HBM) for piece in pieces2]
    fresh = updated(rates, squares, stack, grads)
    middle = by_bit(partner_bits[0], mix, *fresh)

    stack, grads, hidden2, squares = step_pass(pieces2, middle, True)
    blocks = outputs(hidden1, hidden2, weights[2], stack)
    squares, _ = group_sum(squares, blocks)
    fresh = updated(rates, squares, stack, grads)
    new, results = by_bit(partner_bits[1], mix_last, *fresh, *blocks)
    return (new[0].T[None], new[1].T[None], new[2][None], results.reshape(inputs.shape))


def solution(mesh):
    return jax.shard_map(
        local,
        mesh=mesh,
        in_specs=(
            P(None, "replica", "tensor"),
            P(None, "replica", "tensor"),
            P("replica", None, "tensor"),
            P("replica", None, "tensor"),
            P("replica", "tensor", None),
            P("replica"),
            P(),
        ),
        out_specs=(
            P("replica", None, "tensor"),
            P("replica", None, "tensor"),
            P("replica", "tensor", None),
            P(None, "replica", "tensor"),
        ),
        check_vma=False,
    )
```
